128 devices in a mesh: dp: 32 (over x, y_lo, z), gz: 4 (over y_hi, core).
Axes of the slice: x: 4, y: 4 (y_hi: 2, y_lo: 2; y = y_hi * 2 + y_lo), z: 4, core: 2. Of those that a mesh axis runs over, the one named last changes fastest.
Arguments:
- field: bfloat16 [32, 16, 96, 9216], P('dp', None, 'gz'), may hold values from -6 to 6
- cotangent: bfloat16 [32, 16, 96, 9216], P('dp', None, 'gz'), may hold values from -36 to 36, as said below
- spec_weight: float32 [16, 16, 16, 256], P('gz'), may hold values from -1.5 to 1.5
- point_weight: bfloat16 [16, 16], replicated, may hold values from -1.5 to 1.5
- bias: float32 [16], replicated, may hold values from -3 to 3
Outputs:
- field_grad: bfloat16 [32, 16, 96, 9216], P('dp', None, 'gz')
- spectral_grad: float32 [16, 16, 16, 256], P('gz')
- point_grad: float32 [16, 16], replicated
- bias_grad: float32 [16], replicated
The draws below stay inside these ranges and needn't reach their ends.
Inputs may be any that keep to these rules, and one draw needn't show every extreme that they name: `cotangent`: the gradient of the loss with respect to the layer's output.
All inputs are finite; a program needn't handle non-finite values.
Results may differ from the reference program's by a relative error of at most 0.007.
Values sent between devices are 32-bit elements; how exact they have to be, the bound alone decides.
No kernel may reach another device: no remote copies, remote signals or barrier semaphores. Data moves between devices by JAX's collectives and lax.ppermute only.
A program may use at most 192 MiB of HBM per device.

```python
import math
import jax
import jax.numpy as jnp
from jax import lax

N = 96
C = 16
M = 16
SAMPLES = 32


def draw_cotangent(key, part):
    array_shape = (SAMPLES, C, N, N * N)
    sample_pos = jnp.arange(SAMPLES, dtype=jnp.float32) / max(SAMPLES - 1, 1)
    row_pos = jnp.arange(N, dtype=jnp.float32) / (N - 1)
    growth = jnp.exp(math.log(3.0) * sample_pos)[:, None, None, None] * jnp.exp(math.log(3.0) * row_pos)[None, None, :, None]
    raw_values = jnp.clip(jax.random.normal(key, array_shape, jnp.float32), -4.0, 4.0)
    return (raw_values * growth).astype(jnp.bfloat16)


def block_scale(own_key, dims, pieces, smallest, high):
    factor_of, own = 1.0, jax.random.fold_in(own_key, 6)
    for dim, shards_of in pieces:
        draws = jnp.exp(jax.random.uniform(jax.random.fold_in(own, dim), (shards_of,), jnp.float32, smallest / len(pieces), high / len(pieces)))
        factor_of = factor_of * jnp.repeat(draws, dims[dim] // shards_of).reshape([-1 if axis == dim else 1 for axis in range(len(dims))])
    return factor_of


def noise(stream_key, dims, deviation, reach, pieces=(), held_as=jnp.bfloat16):
    entries = deviation * jax.random.normal(stream_key, dims, jnp.float32)
    if pieces:
        entries = entries * block_scale(stream_key, dims, pieces, -0.22, 0.18)
    return jnp.clip(entries, -reach, reach).astype(held_as)


def setup_inputs(seed: int = 0) -> dict:
    seeds = jax.random.split(jax.random.key(seed), 6)
    field = noise(seeds[0], (SAMPLES, C, N, N * N), 1.0, 6.0, ((0, 32), (2, 4)))
    cotangent = draw_cotangent(jax.random.fold_in(seeds[5], 71), 0)
    spec_weight = noise(seeds[2], (M, C, C, M * M), C ** -0.5, 1.5, ((0, 4),), jnp.float32)
    point_weight = noise(seeds[3], (C, C), C ** -0.5, 1.5)
    bias = noise(seeds[4], (C,), 0.5, 3.0, (), jnp.float32)
    return dict(field=field, cotangent=cotangent, spec_weight=spec_weight, point_weight=point_weight, bias=bias)


root_half = 0.7071067811865476
density_norm = 0.3989422804014327

def basis_table(count_modes, length):
    mode_index = jnp.arange(count_modes, dtype=jnp.int32)
    half_count = count_modes // 2
    frequency = jnp.where(mode_index < half_count, mode_index, mode_index - half_count + 1)
    position = jnp.arange(length, dtype=jnp.int32)
    turns = frequency[:, None] * position[None, :] % length
    angle = turns.astype(jnp.float32) * (2.0 * math.pi / length)
    return jnp.where((mode_index < half_count)[:, None], jnp.cos(angle), jnp.sin(angle))

def kron_table(basis):
    outer = basis[:, None, :, None] * basis[None, :, None, :]
    return outer.reshape(M * M, N * N)

def gelu_slope(values):
    cumulative = 0.5 * (1.0 + lax.erf(values * root_half))
    return cumulative + values * jnp.exp(-0.5 * values * values) * density_norm

def reference(field, cotangent, spec_weight, point_weight, bias):
    highest = lax.Precision.HIGHEST
    basis = basis_table(M, N)
    kron = kron_table(basis)
    scale_fwd = (2.0 / N) ** 1.5
    scale_inv = (2.0 / M) ** 1.5
    weight_f = point_weight.astype(jnp.float32)

    def one_sample(carry, pair):
        grad_spec, grad_point, grad_bias = carry
        sample_field, sample_cot = pair
        field_f = sample_field.astype(jnp.float32)
        line = jnp.dot(field_f.reshape(C * N, N * N), kron.T, precision=highest).reshape(C, N, M * M)
        coef = scale_fwd * jnp.einsum('ax,cxp->acp', basis, line, precision=highest)
        mixed = jnp.einsum('aip,aiop->aop', coef, spec_weight, precision=highest)
        inner = jnp.dot(mixed.reshape(M * C, M * M), kron, precision=highest).reshape(M, C, N * N)
        spectral = scale_inv * jnp.einsum('ax,aoz->oxz', basis, inner, precision=highest)
        pre_act = spectral + jnp.einsum('ixz,io->oxz', field_f, weight_f) + bias[:, None, None]
        grad_pre = (sample_cot.astype(jnp.float32) * gelu_slope(pre_act)).astype(jnp.bfloat16)
        grad_pre_f = grad_pre.astype(jnp.float32)
        grad_line = jnp.dot(grad_pre_f.reshape(C * N, N * N), kron.T, precision=highest).reshape(C, N, M * M)
        grad_modes = scale_inv * jnp.einsum('ax,oxp->aop', basis, grad_line, precision=highest)
        grad_spec = grad_spec + jnp.einsum('aip,aop->aiop', coef, grad_modes, precision=highest)
        back_modes = jnp.einsum('aiop,aop->aip', spec_weight, grad_modes, precision=highest)
        back_inner = jnp.dot(back_modes.reshape(M * C, M * M), kron, precision=highest).reshape(M, C, N * N)
        field_grad = scale_fwd * jnp.einsum('ax,aiz->ixz', basis, back_inner, precision=highest)
        field_grad = field_grad + jnp.einsum('oxz,io->ixz', grad_pre_f, weight_f)
        grad_point = grad_point + jnp.einsum('ixz,oxz->io', field_f, grad_pre_f)
        grad_bias = grad_bias + lax.optimization_barrier(jnp.sum(grad_pre_f, axis=(1, 2)))
        return ((grad_spec, grad_point, grad_bias), field_grad.astype(jnp.bfloat16))
    start_state = (jnp.zeros((M, C, C, M * M), jnp.float32), jnp.zeros((C, C), jnp.float32), jnp.zeros((C,), jnp.float32))
    final_state, field_grad = lax.scan(one_sample, start_state, (field, cotangent))
    grad_spec, grad_point, grad_bias = final_state
    cell_norm = math.sqrt(SAMPLES * N * N * N)
    return (field_grad, grad_spec / math.sqrt(SAMPLES * N), grad_point / cell_norm, grad_bias / cell_norm)
```

```python
import functools
import math

import jax
import jax.numpy as jnp
import numpy as np
from jax import lax
from jax.experimental import pallas as pl
from jax.experimental.pallas import tpu as pltpu
from jax.sharding import PartitionSpec as P

N = 96
M = 16
C = 16
GZ = 4
ROWS = N // GZ
CELLS = N * N
MODES = M * M
OWNED = M // GZ * C
SUB = 8

root_half = 0.7071067811865476
density_norm = 0.3989422804014327
scale_fwd = (2.0 / N) ** 1.5
scale_inv = (2.0 / M) ** 1.5
HIGHEST = lax.Precision.HIGHEST
NT = (((1,), (1,)), ((), ()))
TN = (((0,), (0,)), ((), ()))
VMEM_LIMIT = 48 << 20


def basis_table():
    mode_index = np.arange(M)
    half_count = M // 2
    frequency = np.where(mode_index < half_count, mode_index, mode_index - half_count + 1)
    turns = frequency[:, None] * np.arange(N)[None, :] % N
    angle = turns.astype(np.float64) * (2.0 * math.pi / N)
    return np.where((mode_index < half_count)[:, None], np.cos(angle), np.sin(angle)).astype(
        np.float32
    )


def row_matrices(basis):
    out = np.zeros((GZ, M, C, C, ROWS), np.float32)
    for slab in range(GZ):
        for channel in range(C):
            out[slab, :, channel, channel, :] = basis[:, slab * ROWS : (slab + 1) * ROWS]
    return out.reshape(GZ, M * C, C * ROWS)


def gelu_slope(values):
    cumulative = 0.5 * (1.0 + lax.erf(values * root_half))
    return cumulative + values * jnp.exp(-0.5 * values * values) * density_norm


def kron_cells(outer_ref, inner_ref, first, count):
    inner = inner_ref[...]
    parts = [outer_ref[pl.ds(first + k, 1), :] * inner for k in range(count)]
    return jnp.concatenate(parts, 0).astype(jnp.bfloat16)


def one_hot_rows(count, dtype):
    row = lax.broadcasted_iota(jnp.int32, (count * SUB, count), 0) >> 3
    col = lax.broadcasted_iota(jnp.int32, (count * SUB, count), 1)
    return jnp.where(row == col, 1.0, 0.0).astype(dtype)


def same_sub(count):
    row = lax.broadcasted_iota(jnp.int32, (count * SUB, count * SUB), 0) & 7
    col = lax.broadcasted_iota(jnp.int32, (count * SUB, count * SUB), 1) & 7
    return row == col


def spread(weight):
    hot = one_hot_rows(C, jnp.bfloat16)
    tall = jnp.dot(hot, weight, preferred_element_type=jnp.float32).astype(jnp.bfloat16)
    wide = lax.dot_general(tall, hot, NT, preferred_element_type=jnp.float32)
    return jnp.where(same_sub(C), wide, 0.0).astype(jnp.bfloat16)


def send_parts(slab_ref, row_ref, acc, scale, refs):
    for k in range(GZ):
        first = pl.multiple_of((slab_ref[0] ^ k) * OWNED, OWNED)
        rows = row_ref[0, pl.ds(first, OWNED), :]
        refs[k][0:OWNED, :] = scale * jnp.dot(
            rows, acc, precision=HIGHEST, preferred_element_type=jnp.float32
        )


def field_modes_kernel(width, slab_ref, outer_ref, inner_ref, row_ref, field_ref, *rest):
    parts, acc = rest[:GZ], rest[GZ]
    step = pl.program_id(0)

    @pl.when(step == 0)
    def _():
        acc[...] = jnp.zeros_like(acc)

    kron = kron_cells(outer_ref, inner_ref, step * (width // N), width // N)
    acc[...] += jnp.dot(
        field_ref[0].reshape(C * ROWS, width), kron, preferred_element_type=jnp.float32
    )

    @pl.when(step == pl.num_programs(0) - 1)
    def _():
        send_parts(slab_ref, row_ref, acc[...], scale_fwd, parts)


def slope_kernel(
    width,
    sub_width,
    slab_ref,
    outer_ref,
    inner_ref,
    row_ref,
    weight_ref,
    bias_ref,
    mixed_ref,
    field_ref,
    cot_ref,
    dpre_ref,
    *rest,
):
    parts = rest[:GZ]
    lines, blocks, bias_rows, acc, point_acc, kron = rest[GZ:]
    step = pl.program_id(0)

    @pl.when(step == 0)
    def _():
        acc[...] = jnp.zeros_like(acc)
        point_acc[...] = jnp.zeros_like(point_acc)
        full = lax.dot_general(
            row_ref[0], mixed_ref[...], TN, precision=HIGHEST, preferred_element_type=jnp.float32
        )
        lines[...] = (scale_inv * full).reshape(C, ROWS, MODES).astype(jnp.bfloat16)
        blocks[...] = spread(weight_ref[...].T)
        bias_rows[...] = jnp.dot(
            one_hot_rows(C, jnp.float32),
            bias_ref[...],
            precision=HIGHEST,
            preferred_element_type=jnp.float32,
        )

    kron[...] = kron_cells(outer_ref, inner_ref, step * (width // N), width // N)
    for s in range(width // sub_width):
        cols = pl.ds(s * sub_width, sub_width)
        for x in range(ROWS // SUB):
            rows = pl.ds(x * SUB, SUB)
            values = field_ref[0, :, rows, cols].reshape(C * SUB, sub_width)
            pre = lax.dot_general(
                lines[:, rows, :].reshape(C * SUB, MODES),
                kron[cols, :],
                NT,
                preferred_element_type=jnp.float32,
            )
            pre = pre + jnp.dot(blocks[...], values, preferred_element_type=jnp.float32)
            pre = pre + bias_rows[...]
            cot = cot_ref[0, :, rows, cols].reshape(C * SUB, sub_width).astype(jnp.float32)
            dpre = (cot * gelu_slope(pre)).astype(jnp.bfloat16)
            dpre_ref[0, :, rows, cols] = dpre.reshape(C, SUB, sub_width)
    for x in range(ROWS // SUB):
        rows = pl.ds(x * SUB, SUB)
        point_acc[...] += lax.dot_general(
            field_ref[0, :, rows, :].reshape(C * SUB, width),
            dpre_ref[0, :, rows, :].reshape(C * SUB, width),
            NT,
            preferred_element_type=jnp.float32,
        )
    acc[...] += jnp.dot(
        dpre_ref[0].reshape(C * ROWS, width), kron[...], preferred_element_type=jnp.float32
    )

    @pl.when(step == pl.num_programs(0) - 1)
    def _():
        send_parts(slab_ref, row_ref, acc[...], scale_inv, parts)
        hot = one_hot_rows(C, jnp.float32)
        half = jnp.dot(
            jnp.where(same_sub(C), point_acc[...], 0.0),
            hot,
            precision=HIGHEST,
            preferred_element_type=jnp.float32,
        )
        point = lax.dot_general(
            hot, half, TN, precision=HIGHEST, preferred_element_type=jnp.float32
        )
        sums = acc[:, 0:128].reshape(C, ROWS, 128).sum(1)[:, 0:1]
        packed = pack_small(point, sums)
        for k in range(GZ):
            parts[k][OWNED : OWNED + SUB, 0:128] = packed
            parts[k][OWNED : OWNED + SUB, 128:256] = jnp.zeros_like(packed)


def lane_masks():
    row = lax.broadcasted_iota(jnp.int32, (C, 128), 0)
    lane = lax.broadcasted_iota(jnp.int32, (C, 128), 1)
    return row, lane


def pack_small(point, sums):
    row, lane = lane_masks()
    tile = jnp.where((lane & 15) == row, 1.0, 0.0)
    wide = jnp.dot(point, tile, precision=HIGHEST, preferred_element_type=jnp.float32)
    wide = jnp.where((row & 7) == (lane >> 4), wide, 0.0)
    vector = jnp.where(row == lane, sums, 0.0).sum(0, keepdims=True)
    low = wide[0:8].sum(0, keepdims=True)
    high = wide[8:16].sum(0, keepdims=True)
    return jnp.concatenate([low, high, vector, jnp.zeros((5, 128), jnp.float32)], 0)


def unpack_small(packed):
    row, lane = lane_masks()
    wide = jnp.where(row < 8, packed[0:1], packed[1:2])
    wide = jnp.where((row & 7) == (lane >> 4), wide, 0.0)
    tile = jnp.where((lane & 15) == row, 1.0, 0.0)
    point = lax.dot_general(
        wide, tile, NT, precision=HIGHEST, preferred_element_type=jnp.float32
    )
    return point, packed[2:3, 0:C]


def gathered_sum(refs):
    own, one, two, three = (ref[...] for ref in refs)
    return (own + one) + (two + three)


def mix_kernel(own_ref, one_ref, two_ref, three_ref, weight_ref, coef_ref, mixed_ref):
    coef = gathered_sum((own_ref, one_ref, two_ref, three_ref))
    coef_ref[...] = coef
    for a in range(M // GZ):
        total = jnp.zeros((C, MODES), jnp.float32)
        for i in range(C):
            total = total + coef_ref[a * C + i : a * C + i + 1, :] * weight_ref[a, i]
        mixed_ref[a * C : (a + 1) * C, :] = total


def back_kernel(own_ref, one_ref, two_ref, three_ref, weight_ref, coef_ref, back_ref, send_ref):
    full = gathered_sum((own_ref, one_ref, two_ref, three_ref))
    small = full[OWNED : OWNED + SUB]
    for a in range(M // GZ):
        grad = full[a * C : (a + 1) * C]
        for i in range(C):
            back_ref[a * C + i : a * C + i + 1, :] = (weight_ref[a, i] * grad).sum(
                0, keepdims=True
            )
        for pair in range(C // 2):
            owner = a * (C // 2) + pair
            first = a * C + 2 * pair
            send_ref[owner, 0:C, :] = grad
            send_ref[owner, C : C + SUB, :] = jnp.concatenate(
                [coef_ref[first : first + 2, :], small[0:6]], 0
            )


def outer_kernel(spec_norm, cell_norm, got_ref, spread_ref, point_ref, bias_ref):
    samples = got_ref.shape[0]

    def body(s, carry):
        zero, one, small = carry
        grad = got_ref[s, 0:C, :]
        tail = got_ref[s, C : C + SUB, :]
        return zero + tail[0:1] * grad, one + tail[1:2] * grad, small + tail

    start = (
        jnp.zeros((C, MODES), jnp.float32),
        jnp.zeros((C, MODES), jnp.float32),
        jnp.zeros((SUB, MODES), jnp.float32),
    )
    zero, one, small = lax.fori_loop(0, samples, body, start, unroll=8)
    zero = zero * spec_norm
    one = one * spec_norm
    for k in range(samples):
        spread_ref[k, 0] = zero
        spread_ref[k, 1] = one
    point, sums = unpack_small(small[2:8, 0:128])
    point_ref[...] = point * cell_norm
    bias_ref[...] = sums * cell_norm


def field_grad_kernel(
    width,
    sub_width,
    slab_ref,
    outer_ref,
    inner_ref,
    row_ref,
    weight_ref,
    back_ref,
    dpre_ref,
    out_ref,
    lines,
    blocks,
    kron,
):
    step = pl.program_id(0)

    @pl.when(step == 0)
    def _():
        full = lax.dot_general(
            row_ref[0], back_ref[...], TN, precision=HIGHEST, preferred_element_type=jnp.float32
        )
        lines[...] = (scale_fwd * full).reshape(C, ROWS, MODES).astype(jnp.bfloat16)
        blocks[...] = spread(weight_ref[...])

    kron[...] = kron_cells(outer_ref, inner_ref, step * (width // N), width // N)
    for s in range(width // sub_width):
        cols = pl.ds(s * sub_width, sub_width)
        for x in range(ROWS // SUB):
            rows = pl.ds(x * SUB, SUB)
            dpre = dpre_ref[0, :, rows, cols].reshape(C * SUB, sub_width)
            out = lax.dot_general(
                lines[:, rows, :].reshape(C * SUB, MODES),
                kron[cols, :],
                NT,
                preferred_element_type=jnp.float32,
            )
            out = out + jnp.dot(blocks[...], dpre, preferred_element_type=jnp.float32)
            out_ref[0, :, rows, cols] = out.astype(jnp.bfloat16).reshape(C, SUB, sub_width)


def whole(shape):
    return pl.BlockSpec(shape, lambda step, slab: (0,) * len(shape))


def cells(width):
    return pl.BlockSpec((1, C, ROWS, width), lambda step, slab: (0, 0, 0, step))


def slab_rows():
    return pl.BlockSpec((1, M * C, C * ROWS), lambda step, slab: (slab[0], 0, 0))


def f32(*shape):
    return jax.ShapeDtypeStruct(shape, jnp.float32)


params = pltpu.CompilerParams(vmem_limit_bytes=VMEM_LIMIT)


def shards(field, cotangent, spec_weight, point_weight, bias):
    dp = lax.axis_size("dp")
    basis = basis_table()
    slab = lax.axis_index("gz").astype(jnp.int32).reshape(1)
    outer_rows = jnp.asarray(np.repeat(basis.T, M, axis=1))
    inner_rows = jnp.asarray(np.tile(basis.T, (1, M)))
    row_mats = jnp.asarray(row_matrices(basis))

    def exchange(parts):
        got = [parts[0]]
        for k in range(1, GZ):
            got.append(lax.ppermute(parts[k], "gz", [(g, g ^ k) for g in range(GZ)]))
        return got

    width = 2304
    coef_parts = pl.pallas_call(
        functools.partial(field_modes_kernel, width),
        out_shape=tuple(f32(OWNED, MODES) for _ in range(GZ)),
        grid_spec=pltpu.PrefetchScalarGridSpec(
            num_scalar_prefetch=1,
            grid=(CELLS // width,),
            in_specs=[whole((N, MODES)), whole((N, MODES)), slab_rows(), cells(width)],
            out_specs=tuple(whole((OWNED, MODES)) for _ in range(GZ)),
            scratch_shapes=[pltpu.VMEM((C * ROWS, MODES), jnp.float32)],
        ),
        compiler_params=params,
        name="field_modes",
    )(slab, outer_rows, inner_rows, row_mats, field)

    coef, mixed = pl.pallas_call(
        mix_kernel,
        out_shape=(f32(OWNED, MODES), f32(OWNED, MODES)),
        compiler_params=params,
        name="mix_modes",
    )(*exchange(coef_parts), spec_weight)
    mixed_all = lax.all_gather(mixed, "gz", axis=0, tiled=True)

    width = 1152
    dpre, *grad_parts = pl.pallas_call(
        functools.partial(slope_kernel, width, 384),
        out_shape=(jax.ShapeDtypeStruct(field.shape, jnp.bfloat16),)
        + tuple(f32(OWNED + SUB, MODES) for _ in range(GZ)),
        grid_spec=pltpu.PrefetchScalarGridSpec(
            num_scalar_prefetch=1,
            grid=(CELLS // width,),
            in_specs=[
                whole((N, MODES)),
                whole((N, MODES)),
                slab_rows(),
                whole((C, C)),
                whole((C, 1)),
                whole((M * C, MODES)),
                cells(width),
                cells(width),
            ],
            out_specs=(cells(width),) + tuple(whole((OWNED + SUB, MODES)) for _ in range(GZ)),
            scratch_shapes=[
                pltpu.VMEM((C, ROWS, MODES), jnp.bfloat16),
                pltpu.VMEM((C * SUB, C * SUB), jnp.bfloat16),
                pltpu.VMEM((C * SUB, 1), jnp.float32),
                pltpu.VMEM((C * ROWS, MODES), jnp.float32),
                pltpu.VMEM((C * SUB, C * SUB), jnp.float32),
                pltpu.VMEM((width, MODES), jnp.bfloat16),
            ],
        ),
        compiler_params=params,
        name="slope_and_modes",
    )(
        slab,
        outer_rows,
        inner_rows,
        row_mats,
        point_weight,
        bias.reshape(C, 1),
        mixed_all,
        field,
        cotangent,
    )

    back, send = pl.pallas_call(
        back_kernel,
        out_shape=(f32(OWNED, MODES), f32(dp, C + SUB, MODES)),
        compiler_params=params,
        name="back_modes",
    )(*exchange(grad_parts), spec_weight, coef)

    got = lax.all_to_all(send, "dp", 0, 0, tiled=True)
    cell_norm = 1.0 / math.sqrt(dp * N * N * N)
    copies, point_grad, bias_grad = pl.pallas_call(
        functools.partial(outer_kernel, 1.0 / math.sqrt(dp * N), cell_norm),
        out_shape=(f32(dp, 2, C, MODES), f32(C, C), f32(1, C)),
        compiler_params=params,
        name="sample_sum",
    )(got)
    spec_grad = lax.all_to_all(copies, "dp", 0, 0, tiled=True)

    back_all = lax.all_gather(back, "gz", axis=0, tiled=True)
    width = 2304
    field_grad = pl.pallas_call(
        functools.partial(field_grad_kernel, width, 384),
        out_shape=jax.ShapeDtypeStruct(field.shape, jnp.bfloat16),
        grid_spec=pltpu.PrefetchScalarGridSpec(
            num_scalar_prefetch=1,
            grid=(CELLS // width,),
            in_specs=[
                whole((N, MODES)),
                whole((N, MODES)),
                slab_rows(),
                whole((C, C)),
                whole((M * C, MODES)),
                cells(width),
            ],
            out_specs=cells(width),
            scratch_shapes=[
                pltpu.VMEM((C, ROWS, MODES), jnp.bfloat16),
                pltpu.VMEM((C * SUB, C * SUB), jnp.bfloat16),
                pltpu.VMEM((width, MODES), jnp.bfloat16),
            ],
        ),
        compiler_params=params,
        name="field_grad",
    )(slab, outer_rows, inner_rows, row_mats, point_weight, back_all, dpre)

    return (
        field_grad,
        spec_grad.reshape(M // GZ, C, C, MODES),
        point_grad,
        bias_grad.reshape(C),
    )


def solution(mesh):
    return jax.shard_map(
        shards,
        mesh=mesh,
        in_specs=(
            P("dp", None, "gz", None),
            P("dp", None, "gz", None),
            P("gz", None, None, None),
            P(),
            P(),
        ),
        out_specs=(P("dp", None, "gz", None), P("gz", None, None, None), P(), P()),
        check_vma=False,
    )
```

```python
import functools
import math

import jax
import jax.numpy as jnp
from jax import lax
from jax.experimental import pallas as pl
from jax.experimental.pallas import tpu as pltpu
from jax.sharding import PartitionSpec as P

N = 96
M = 16
C = 16
GZ = 4
ROWS = N // GZ
CELLS = N * N
MODES = M * M
OWNED = M // GZ * C
SUB = 8
LANES = 128
CHUNKS = 6
WIDTH = CELLS // CHUNKS

bf16 = jnp.bfloat16
root_half = 0.7071067811865476
density_norm = 0.3989422804014327
scale_fwd = (2.0 / N) ** 1.5
scale_inv = (2.0 / M) ** 1.5
HIGHEST = lax.Precision.HIGHEST
NN = (((1,), (0,)), ((), ()))
NT = (((1,), (1,)), ((), ()))
TN = (((0,), (0,)), ((), ()))


def gelu_slope(values):
    cumulative = 0.5 * (1.0 + lax.erf(values * root_half))
    return cumulative + values * jnp.exp(-0.5 * values * values) * density_norm


def matmul(a, b, dims=NN):
    return lax.dot_general(a, b, dims, preferred_element_type=jnp.float32)


def split(values):
    high = values.astype(bf16)
    return high, (values - high.astype(jnp.float32)).astype(bf16)


def product(a, b, dims):
    return matmul(a[0], b[0], dims) + (matmul(a[0], b[1], dims) + matmul(a[1], b[0], dims))


def iota(shape, dim):
    return lax.broadcasted_iota(jnp.int32, shape, dim)


def quotient(values, divisor):
    return jnp.floor((values + 0.5) * (1.0 / divisor))


def basis_at(mode, position):
    cosine = mode < M // 2
    frequency = jnp.where(cosine, mode, mode - (M // 2 - 1))
    turns = frequency * position + jnp.where(cosine, 0.0, 0.75 * N)
    turns = turns - N * quotient(turns, N)
    return jnp.cos(turns * (2.0 * math.pi / N))


def cell_tables():
    mode = iota((N, MODES), 1)
    cell = iota((N, MODES), 0).astype(jnp.float32)
    outer = basis_at((mode >> 4).astype(jnp.float32), cell)
    return outer, basis_at((mode & 15).astype(jnp.float32), cell)


def row_matrix(slab):
    col = iota((M, C * ROWS), 1).astype(jnp.float32)
    x = col - ROWS * quotient(col, ROWS) + (slab * ROWS).astype(jnp.float32)
    table = basis_at(iota((M, C * ROWS), 0).astype(jnp.float32), x)
    wide = jnp.broadcast_to(table[:, None, :], (M, C, C * ROWS)).reshape(M * C, C * ROWS)
    row_channel = (iota((M * C, C * ROWS), 0) & 15).astype(jnp.float32)
    col_channel = quotient(iota((M * C, C * ROWS), 1).astype(jnp.float32), ROWS)
    return jnp.where(row_channel == col_channel, wide, 0.0)


def one_hot_rows(dtype):
    hit = (iota((C * SUB, C), 0) >> 3) == iota((C * SUB, C), 1)
    return jnp.where(hit, 1.0, 0.0).astype(dtype)


def same_sub():
    return (iota((C * SUB, C * SUB), 0) & 7) == (iota((C * SUB, C * SUB), 1) & 7)


def spread(weight):
    hot = one_hot_rows(bf16)
    tall = matmul(hot, weight).astype(bf16)
    return jnp.where(same_sub(), matmul(tall, hot, NT), 0.0).astype(bf16)


def send_parts(slab, high_ref, low_ref, acc, scale, refs):
    pair = split(acc)
    for k in range(GZ):
        first = pl.multiple_of((slab ^ k) * OWNED, OWNED)
        rows = (high_ref[pl.ds(first, OWNED), :], low_ref[pl.ds(first, OWNED), :])
        refs[k][0:OWNED, :] = scale * product(rows, pair, NN)


def chunk(step):
    return pl.ds(pl.multiple_of(step * WIDTH, LANES), WIDTH)


def copies_in(source, target, sems):
    def copy(step):
        cols = chunk(step)
        return pltpu.make_async_copy(
            source.at[0, :, :, cols], target.at[:, :, cols], sems.at[step]
        )

    return copy


def copies_out(source, target, sems):
    def copy(step):
        cols = chunk(step)
        return pltpu.make_async_copy(
            source.at[:, :, cols], target.at[0, :, :, cols], sems.at[step]
        )

    return copy


def kron_rows(outer, inner, step):
    table = inner[...]
    rows = [
        (outer[pl.ds(step * (WIDTH // N) + k, 1), :] * table).astype(bf16)
        for k in range(WIDTH // N)
    ]
    return jnp.concatenate(rows, 0)


def field_modes_kernel(slab_ref, field_hbm, *rest):
    parts = rest[:GZ]
    outer, inner, high, low, field, acc, sems = rest[GZ:]
    fetch = copies_in(field_hbm, field, sems)
    for step in range(CHUNKS):
        fetch(step).start()
    outer[...], inner[...] = cell_tables()
    high[...], low[...] = split(row_matrix(slab_ref[0]))
    acc[...] = jnp.zeros_like(acc)

    def body(step, carry):
        kron = kron_rows(outer, inner, step)
        fetch(step).wait()
        acc[...] += matmul(field[:, :, chunk(step)].reshape(C * ROWS, WIDTH), kron)
        return carry

    lax.fori_loop(0, CHUNKS, body, 0)
    send_parts(slab_ref[0], high, low, acc[...], scale_fwd, parts)


def slope_kernel(
    sub_width,
    slab_ref,
    field_hbm,
    cot_hbm,
    outer,
    inner,
    high,
    low,
    weight_ref,
    bias_ref,
    mixed_ref,
    dpre_hbm,
    *rest,
):
    parts = rest[:GZ]
    down, bias_rows, field, cot, out, lines, acc, point_acc, kron, kron_t, *sems = rest[GZ:]
    field_sems, cot_sems, out_sems = sems
    fetch_field = copies_in(field_hbm, field, field_sems)
    fetch_cot = copies_in(cot_hbm, cot, cot_sems)
    store = copies_out(out, dpre_hbm, out_sems)
    for step in range(CHUNKS):
        fetch_field(step).start()
        fetch_cot(step).start()
    down[...] = spread(weight_ref[...].T)
    bias_rows[...] = jnp.dot(
        one_hot_rows(jnp.float32),
        bias_ref[...],
        precision=HIGHEST,
        preferred_element_type=jnp.float32,
    )
    full = product((high[...], low[...]), split(mixed_ref[...]), TN)
    lines[...] = (scale_inv * full).reshape(C, ROWS, MODES).astype(bf16)
    acc[...] = jnp.zeros_like(acc)
    point_acc[...] = jnp.zeros_like(point_acc)

    def body(step, carry):
        kron[...] = kron_rows(outer, inner, step)
        kron_t[...] = kron[...].T
        fetch_field(step).wait()
        fetch_cot(step).wait()
        for s in range(WIDTH // sub_width):
            cols = pl.ds(pl.multiple_of(step * WIDTH + s * sub_width, LANES), sub_width)
            table = kron_t[:, s * sub_width : (s + 1) * sub_width]
            for x in range(ROWS // SUB):
                rows = slice(x * SUB, (x + 1) * SUB)
                values = field[:, rows, cols].reshape(C * SUB, sub_width)
                left = jnp.concatenate([lines[:, rows, :].reshape(C * SUB, MODES), down[...]], 1)
                pre = matmul(left, jnp.concatenate([table, values], 0))
                pre = pre + bias_rows[...]
                grad = cot[:, rows, cols].reshape(C * SUB, sub_width).astype(jnp.float32)
                dpre = (grad * gelu_slope(pre)).astype(bf16)
                out[:, rows, cols] = dpre.reshape(C, SUB, sub_width)
        store(step).start()
        cols = chunk(step)
        for x in range(ROWS // SUB):
            rows = slice(x * SUB, (x + 1) * SUB)
            point_acc[...] += matmul(
                field[:, rows, cols].reshape(C * SUB, WIDTH),
                out[:, rows, cols].reshape(C * SUB, WIDTH),
                NT,
            )
        acc[...] += matmul(out[:, :, cols].reshape(C * ROWS, WIDTH), kron[...])
        return carry

    lax.fori_loop(0, CHUNKS, body, 0)
    send_parts(slab_ref[0], high, low, acc[...], scale_inv, parts)
    hot = one_hot_rows(jnp.float32)
    half = jnp.dot(
        jnp.where(same_sub(), point_acc[...], 0.0),
        hot,
        precision=HIGHEST,
        preferred_element_type=jnp.float32,
    )
    point = lax.dot_general(hot, half, TN, precision=HIGHEST, preferred_element_type=jnp.float32)
    sums = acc[:, 0:LANES].reshape(C, ROWS, LANES).sum(1)[:, 0:1]
    packed = pack_small(point, sums)
    for k in range(GZ):
        parts[k][OWNED : OWNED + SUB, 0:LANES] = packed
        parts[k][OWNED : OWNED + SUB, LANES:MODES] = jnp.zeros_like(packed)
    for step in range(CHUNKS):
        store(step).wait()


def lane_masks():
    return iota((C, LANES), 0), iota((C, LANES), 1)


def pack_small(point, sums):
    row, lane = lane_masks()
    tile = jnp.where((lane & 15) == row, 1.0, 0.0)
    wide = jnp.dot(point, tile, precision=HIGHEST, preferred_element_type=jnp.float32)
    wide = jnp.where((row & 7) == (lane >> 4), wide, 0.0)
    vector = jnp.where(row == lane, sums, 0.0).sum(0, keepdims=True)
    low = wide[0:8].sum(0, keepdims=True)
    high = wide[8:16].sum(0, keepdims=True)
    return jnp.concatenate([low, high, vector, jnp.zeros((5, LANES), jnp.float32)], 0)


def unpack_small(packed):
    row, lane = lane_masks()
    wide = jnp.where(row < 8, packed[0:1], packed[1:2])
    wide = jnp.where((row & 7) == (lane >> 4), wide, 0.0)
    tile = jnp.where((lane & 15) == row, 1.0, 0.0)
    point = lax.dot_general(wide, tile, NT, precision=HIGHEST, preferred_element_type=jnp.float32)
    return point, packed[2:3, 0:C]


def gathered_sum(refs):
    own, one, two, three = (ref[...] for ref in refs)
    return (own + one) + (two + three)


def mix_kernel(own_ref, one_ref, two_ref, three_ref, weight_ref, coef_ref, mixed_ref):
    coef = gathered_sum((own_ref, one_ref, two_ref, three_ref))
    coef_ref[...] = coef
    for a in range(M // GZ):
        total = jnp.zeros((C, MODES), jnp.float32)
        for i in range(C):
            total = total + coef_ref[a * C + i : a * C + i + 1, :] * weight_ref[a, i]
        mixed_ref[a * C : (a + 1) * C, :] = total


def pieces():
    for owner in range(M // GZ * 8):
        yield owner, owner // 8, owner // 4 % 2 * SUB, owner // 2 % 2 * SUB, owner % 2 * LANES


def back_kernel(own_ref, one_ref, two_ref, three_ref, weight_ref, coef_ref, back_ref, send_ref):
    full = gathered_sum((own_ref, one_ref, two_ref, three_ref))
    small = full[OWNED : OWNED + SUB, 0:LANES]
    for owner, a, i, o, p in pieces():
        send_ref[owner, 0:SUB, :] = coef_ref[a * C + i : a * C + i + SUB, p : p + LANES]
        send_ref[owner, SUB : 2 * SUB, :] = full[a * C + o : a * C + o + SUB, p : p + LANES]
        send_ref[owner, 2 * SUB : 3 * SUB, :] = small
    for a in range(M // GZ):
        grad = full[a * C : (a + 1) * C]
        for i in range(C):
            back_ref[a * C + i : a * C + i + 1, :] = (weight_ref[a, i] * grad).sum(
                0, keepdims=True
            )


def outer_kernel(spec_norm, cell_norm, got_ref, copies_ref, point_ref, bias_ref):
    samples = got_ref.shape[0]

    def body(s, carry):
        *totals, small = carry
        coef = got_ref[s, 0:SUB, :]
        grad = got_ref[s, SUB : 2 * SUB, :]
        totals = [total + coef[i : i + 1] * grad for i, total in enumerate(totals)]
        return (*totals, small + got_ref[s, 2 * SUB : 3 * SUB, :])

    zero = jnp.zeros((SUB, LANES), jnp.float32)
    *totals, small = lax.fori_loop(0, samples, body, (zero,) * (SUB + 1), unroll=8)
    for i, total in enumerate(totals):
        scaled = total * spec_norm
        for k in range(samples):
            copies_ref[k, i] = scaled
    point, sums = unpack_small(small)
    point_ref[...] = point * cell_norm
    bias_ref[...] = sums * cell_norm


def place_kernel(got_ref, out_ref):
    for owner, a, i, o, p in pieces():
        out_ref[a, i : i + SUB, o : o + SUB, p : p + LANES] = got_ref[owner]


def field_grad_kernel(
    sub_width,
    dpre_hbm,
    outer,
    inner,
    high,
    low,
    weight_ref,
    back_ref,
    out_hbm,
    up,
    dpre,
    out,
    lines,
    kron_t,
    dpre_sems,
    out_sems,
):
    fetch = copies_in(dpre_hbm, dpre, dpre_sems)
    store = copies_out(out, out_hbm, out_sems)
    for step in range(CHUNKS):
        fetch(step).start()
    up[...] = spread(weight_ref[...])
    full = product((high[...], low[...]), split(back_ref[...]), TN)
    lines[...] = (scale_fwd * full).reshape(C, ROWS, MODES).astype(bf16)

    def body(step, carry):
        kron_t[...] = kron_rows(outer, inner, step).T
        fetch(step).wait()
        for s in range(WIDTH // sub_width):
            cols = pl.ds(pl.multiple_of(step * WIDTH + s * sub_width, LANES), sub_width)
            table = kron_t[:, s * sub_width : (s + 1) * sub_width]
            for x in range(ROWS // SUB):
                rows = slice(x * SUB, (x + 1) * SUB)
                values = dpre[:, rows, cols].reshape(C * SUB, sub_width)
                left = jnp.concatenate([lines[:, rows, :].reshape(C * SUB, MODES), up[...]], 1)
                grad = matmul(left, jnp.concatenate([table, values], 0))
                out[:, rows, cols] = grad.astype(bf16).reshape(C, SUB, sub_width)
        store(step).start()
        return carry

    lax.fori_loop(0, CHUNKS, body, 0)
    for step in range(CHUNKS):
        store(step).wait()


def shaped(*shape, dtype=jnp.float32):
    return jax.ShapeDtypeStruct(shape, dtype)


def limit(mebibytes):
    return pltpu.CompilerParams(vmem_limit_bytes=mebibytes << 20)


VM = pl.BlockSpec(memory_space=pltpu.VMEM)
SM = pl.BlockSpec(memory_space=pltpu.SMEM)
ANY = pl.BlockSpec(memory_space=pl.ANY)


def shards(field, cotangent, spec_weight, point_weight, bias):
    dp = lax.axis_size("dp")
    slab = lax.axis_index("gz").astype(jnp.int32).reshape(1)

    def exchange(parts):
        got = [parts[0]]
        for k in range(1, GZ):
            got.append(lax.ppermute(parts[k], "gz", [(g, g ^ k) for g in range(GZ)]))
        return got

    *coef_parts, outer, inner, high, low = pl.pallas_call(
        field_modes_kernel,
        out_shape=tuple(shaped(OWNED, MODES) for _ in range(GZ))
        + (
            shaped(N, MODES),
            shaped(N, MODES),
            shaped(M * C, C * ROWS, dtype=bf16),
            shaped(M * C, C * ROWS, dtype=bf16),
        ),
        in_specs=[SM, ANY],
        out_specs=(VM,) * (GZ + 4),
        scratch_shapes=[
            pltpu.VMEM((C, ROWS, CELLS), bf16),
            pltpu.VMEM((C * ROWS, MODES), jnp.float32),
            pltpu.SemaphoreType.DMA((CHUNKS,)),
        ],
        compiler_params=limit(53),
        name="field_modes",
    )(slab, field)

    coef, mixed = pl.pallas_call(
        mix_kernel,
        out_shape=(shaped(OWNED, MODES), shaped(OWNED, MODES)),
        compiler_params=limit(8),
        name="mix_modes",
    )(*exchange(coef_parts), spec_weight)
    mixed_all = lax.all_gather(mixed, "gz", axis=0, tiled=True)

    dpre, *grad_parts = pl.pallas_call(
        functools.partial(slope_kernel, 768),
        out_shape=(jax.ShapeDtypeStruct(field.shape, bf16),)
        + tuple(shaped(OWNED + SUB, MODES) for _ in range(GZ)),
        in_specs=[SM, ANY, ANY] + [VM] * 7,
        out_specs=(ANY,) + (VM,) * GZ,
        scratch_shapes=[
            pltpu.VMEM((C * SUB, C * SUB), bf16),
            pltpu.VMEM((C * SUB, 1), jnp.float32),
            pltpu.VMEM((C, ROWS, CELLS), bf16),
            pltpu.VMEM((C, ROWS, CELLS), bf16),
            pltpu.VMEM((C, ROWS, CELLS), bf16),
            pltpu.VMEM((C, ROWS, MODES), bf16),
            pltpu.VMEM((C * ROWS, MODES), jnp.float32),
            pltpu.VMEM((C * SUB, C * SUB), jnp.float32),
            pltpu.VMEM((WIDTH, MODES), bf16),
            pltpu.VMEM((MODES, WIDTH), bf16),
            pltpu.SemaphoreType.DMA((CHUNKS,)),
            pltpu.SemaphoreType.DMA((CHUNKS,)),
            pltpu.SemaphoreType.DMA((CHUNKS,)),
        ],
        compiler_params=limit(53),
        name="slope_and_modes",
    )(
        slab,
        field,
        cotangent,
        outer,
        inner,
        high,
        low,
        point_weight,
        bias.reshape(C, 1),
        mixed_all,
    )

    back, send = pl.pallas_call(
        back_kernel,
        out_shape=(shaped(OWNED, MODES), shaped(dp, 3 * SUB, LANES)),
        compiler_params=limit(8),
        name="back_modes",
    )(*exchange(grad_parts), spec_weight, coef)

    got = lax.all_to_all(send, "dp", 0, 0, tiled=True)
    back_all = lax.all_gather(back, "gz", axis=0, tiled=True)
    got, back_all = lax.optimization_barrier((got, back_all))
    copies, point_grad, bias_grad = pl.pallas_call(
        functools.partial(
            outer_kernel, 1.0 / math.sqrt(dp * N), 1.0 / math.sqrt(dp * N * N * N)
        ),
        out_shape=(shaped(dp, SUB, SUB, LANES), shaped(C, C), shaped(1, C)),
        compiler_params=limit(8),
        name="sample_sum",
    )(got)
    owned = lax.all_to_all(copies, "dp", 0, 0, tiled=True)

    field_grad = pl.pallas_call(
        functools.partial(field_grad_kernel, 768),
        out_shape=jax.ShapeDtypeStruct(field.shape, bf16),
        in_specs=[ANY] + [VM] * 6,
        out_specs=ANY,
        scratch_shapes=[
            pltpu.VMEM((C * SUB, C * SUB), bf16),
            pltpu.VMEM((C, ROWS, CELLS), bf16),
            pltpu.VMEM((C, ROWS, CELLS), bf16),
            pltpu.VMEM((C, ROWS, MODES), bf16),
            pltpu.VMEM((MODES, WIDTH), bf16),
            pltpu.SemaphoreType.DMA((CHUNKS,)),
            pltpu.SemaphoreType.DMA((CHUNKS,)),
        ],
        compiler_params=limit(54),
        cost_estimate=pl.CostEstimate(
            flops=2 * C * ROWS * CELLS * (MODES + C * SUB),
            bytes_accessed=2 * C * ROWS * CELLS * 2,
            transcendentals=0,
        ),
        name="field_grad",
    )(dpre, outer, inner, high, low, point_weight, back_all)

    spec_grad = pl.pallas_call(
        place_kernel,
        out_shape=shaped(M // GZ, C, C, MODES),
        compiler_params=limit(8),
        name="place_pieces",
    )(owned)
    return field_grad, spec_grad, point_grad, bias_grad.reshape(C)


def solution(mesh):
    return jax.shard_map(
        shards,
        mesh=mesh,
        in_specs=(
            P("dp", None, "gz", None),
            P("dp", None, "gz", None),
            P("gz", None, None, None),
            P(),
            P(),
        ),
        out_specs=(P("dp", None, "gz", None), P("gz", None, None, None), P(), P()),
        check_vma=False,
    )
```

```python
import functools
import math

import jax
import jax.numpy as jnp
from jax import lax
from jax.experimental import pallas as pl
from jax.experimental.pallas import tpu as pltpu
from jax.sharding import PartitionSpec as P

N = 96
M = 16
C = 16
GZ = 4
ROWS = N // GZ
CELLS = N * N
MODES = M * M
OWNED = M // GZ * C
SUB = 8
LANES = 128
CHUNKS = 6
WIDTH = CELLS // CHUNKS

bf16 = jnp.bfloat16
root_half = 0.7071067811865476
density_norm = 0.3989422804014327
scale_fwd = (2.0 / N) ** 1.5
scale_inv = (2.0 / M) ** 1.5
HIGHEST = lax.Precision.HIGHEST
NN = (((1,), (0,)), ((), ()))
NT = (((1,), (1,)), ((), ()))
TN = (((0,), (0,)), ((), ()))


def gelu_slope(values):
    cumulative = 0.5 * (1.0 + lax.erf(values * root_half))
    return cumulative + values * jnp.exp(-0.5 * values * values) * density_norm


def matmul(a, b, dims=NN):
    return lax.dot_general(a, b, dims, preferred_element_type=jnp.float32)


def split(values):
    high = values.astype(bf16)
    return high, (values - high.astype(jnp.float32)).astype(bf16)


def product(a, b, dims):
    return matmul(a[0], b[0], dims) + (matmul(a[0], b[1], dims) + matmul(a[1], b[0], dims))


def iota(shape, dim):
    return lax.broadcasted_iota(jnp.int32, shape, dim)


def quotient(values, divisor):
    return jnp.floor((values + 0.5) * (1.0 / divisor))


def basis_at(mode, position):
    cosine = mode < M // 2
    frequency = jnp.where(cosine, mode, mode - (M // 2 - 1))
    turns = frequency * position + jnp.where(cosine, 0.0, 0.75 * N)
    turns = turns - N * quotient(turns, N)
    return jnp.cos(turns * (2.0 * math.pi / N))


def cell_tables():
    mode = iota((N, MODES), 1)
    cell = iota((N, MODES), 0).astype(jnp.float32)
    outer = basis_at((mode >> 4).astype(jnp.float32), cell)
    return outer, basis_at((mode & 15).astype(jnp.float32), cell)


def row_matrix(slab):
    col = iota((M, C * ROWS), 1).astype(jnp.float32)
    x = col - ROWS * quotient(col, ROWS) + (slab * ROWS).astype(jnp.float32)
    table = basis_at(iota((M, C * ROWS), 0).astype(jnp.float32), x)
    wide = jnp.broadcast_to(table[:, None, :], (M, C, C * ROWS)).reshape(M * C, C * ROWS)
    row_channel = (iota((M * C, C * ROWS), 0) & 15).astype(jnp.float32)
    col_channel = quotient(iota((M * C, C * ROWS), 1).astype(jnp.float32), ROWS)
    return jnp.where(row_channel == col_channel, wide, 0.0)


def one_hot_rows(dtype):
    hit = (iota((C * SUB, C), 0) >> 3) == iota((C * SUB, C), 1)
    return jnp.where(hit, 1.0, 0.0).astype(dtype)


def same_sub():
    return (iota((C * SUB, C * SUB), 0) & 7) == (iota((C * SUB, C * SUB), 1) & 7)


def spread(weight):
    hot = one_hot_rows(bf16)
    tall = matmul(hot, weight).astype(bf16)
    return jnp.where(same_sub(), matmul(tall, hot, NT), 0.0).astype(bf16)


def send_parts(slab, high_ref, low_ref, acc, scale, refs):
    pair = split(acc)
    for k in range(GZ):
        first = pl.multiple_of((slab ^ k) * OWNED, OWNED)
        rows = (high_ref[pl.ds(first, OWNED), :], low_ref[pl.ds(first, OWNED), :])
        refs[k][0:OWNED, :] = scale * product(rows, pair, NN)


def chunk(step):
    return slice(step * WIDTH, (step + 1) * WIDTH)


def copies_in(source, target, sems):
    def copy(step):
        cols = chunk(step)
        return pltpu.make_async_copy(
            source.at[0, :, :, cols], target.at[:, :, cols], sems.at[step]
        )

    return copy


def copies_out(source, target, sems):
    def copy(step):
        cols = chunk(step)
        return pltpu.make_async_copy(
            source.at[:, :, cols], target.at[0, :, :, cols], sems.at[step]
        )

    return copy


def kron_rows(outer, inner, step):
    table = inner[...]
    rows = [
        (outer[step * (WIDTH // N) + k : step * (WIDTH // N) + k + 1, :] * table).astype(bf16)
        for k in range(WIDTH // N)
    ]
    return jnp.concatenate(rows, 0)


def field_modes_kernel(slab_ref, field_hbm, *rest):
    parts = rest[:GZ]
    outer, inner, high, low, field, acc, sems = rest[GZ:]
    fetch = copies_in(field_hbm, field, sems)
    for step in range(CHUNKS):
        fetch(step).start()
    outer[...], inner[...] = cell_tables()
    high[...], low[...] = split(row_matrix(slab_ref[0]))
    acc[...] = jnp.zeros_like(acc)

    for step in range(CHUNKS):
        kron = kron_rows(outer, inner, step)
        fetch(step).wait()
        acc[...] += matmul(field[:, :, chunk(step)].reshape(C * ROWS, WIDTH), kron)
    send_parts(slab_ref[0], high, low, acc[...], scale_fwd, parts)


def slope_kernel(
    sub_width,
    slab_ref,
    field_hbm,
    cot_hbm,
    outer,
    inner,
    high,
    low,
    weight_ref,
    bias_ref,
    mixed_ref,
    dpre_hbm,
    *rest,
):
    parts = rest[:GZ]
    down, bias_cols, field, cot, out, lines, acc, point_acc, kron, kron_t, *sems = rest[GZ:]
    field_sems, cot_sems, out_sems = sems
    fetch_field = copies_in(field_hbm, field, field_sems)
    fetch_cot = copies_in(cot_hbm, cot, cot_sems)
    store = copies_out(out, dpre_hbm, out_sems)
    for step in range(CHUNKS):
        fetch_field(step).start()
        fetch_cot(step).start()
    down[...] = spread(weight_ref[...].T)
    bias_high, bias_low = split(
        jnp.dot(
            one_hot_rows(jnp.float32),
            bias_ref[...],
            precision=HIGHEST,
            preferred_element_type=jnp.float32,
        )
    )
    lane = iota((C * SUB, C), 1)
    bias_cols[...] = jnp.where(
        lane == 0,
        bias_high.astype(jnp.float32),
        jnp.where(lane == 1, bias_low.astype(jnp.float32), 0.0),
    ).astype(bf16)
    ones = jnp.ones((C, sub_width), bf16)
    full = product((high[...], low[...]), split(mixed_ref[...]), TN)
    lines[...] = (scale_inv * full).reshape(C, ROWS, MODES).astype(bf16)
    acc[...] = jnp.zeros_like(acc)
    point_acc[...] = jnp.zeros_like(point_acc)

    for step in range(CHUNKS):
        kron[...] = kron_rows(outer, inner, step)
        kron_t[...] = kron[...].T
        fetch_field(step).wait()
        fetch_cot(step).wait()
        for s in range(WIDTH // sub_width):
            cols = slice(step * WIDTH + s * sub_width, step * WIDTH + (s + 1) * sub_width)
            table = kron_t[:, s * sub_width : (s + 1) * sub_width]
            for x in range(ROWS // SUB):
                rows = slice(x * SUB, (x + 1) * SUB)
                values = field[:, rows, cols].reshape(C * SUB, sub_width)
                left = jnp.concatenate(
                    [lines[:, rows, :].reshape(C * SUB, MODES), down[...], bias_cols[...]], 1
                )
                pre = matmul(left, jnp.concatenate([table, values, ones], 0))
                grad = cot[:, rows, cols].reshape(C * SUB, sub_width).astype(jnp.float32)
                dpre = (grad * gelu_slope(pre)).astype(bf16)
                out[:, rows, cols] = dpre.reshape(C, SUB, sub_width)
        store(step).start()
        cols = chunk(step)
        for x in range(ROWS // SUB):
            rows = slice(x * SUB, (x + 1) * SUB)
            point_acc[...] += matmul(
                field[:, rows, cols].reshape(C * SUB, WIDTH),
                out[:, rows, cols].reshape(C * SUB, WIDTH),
                NT,
            )
        acc[...] += matmul(out[:, :, cols].reshape(C * ROWS, WIDTH), kron[...])
    send_parts(slab_ref[0], high, low, acc[...], scale_inv, parts)
    hot = one_hot_rows(jnp.float32)
    half = jnp.dot(
        jnp.where(same_sub(), point_acc[...], 0.0),
        hot,
        precision=HIGHEST,
        preferred_element_type=jnp.float32,
    )
    point = lax.dot_general(hot, half, TN, precision=HIGHEST, preferred_element_type=jnp.float32)
    sums = acc[:, 0:LANES].reshape(C, ROWS, LANES).sum(1)[:, 0:1]
    packed = pack_small(point, sums)
    for k in range(GZ):
        parts[k][OWNED : OWNED + SUB, 0:LANES] = packed
        parts[k][OWNED : OWNED + SUB, LANES:MODES] = jnp.zeros_like(packed)
    for step in range(CHUNKS):
        store(step).wait()


def lane_masks():
    return iota((C, LANES), 0), iota((C, LANES), 1)


def pack_small(point, sums):
    row, lane = lane_masks()
    tile = jnp.where((lane & 15) == row, 1.0, 0.0)
    wide = jnp.dot(point, tile, precision=HIGHEST, preferred_element_type=jnp.float32)
    wide = jnp.where((row & 7) == (lane >> 4), wide, 0.0)
    vector = jnp.where(row == lane, sums, 0.0).sum(0, keepdims=True)
    low = wide[0:8].sum(0, keepdims=True)
    high = wide[8:16].sum(0, keepdims=True)
    return jnp.concatenate([low, high, vector, jnp.zeros((5, LANES), jnp.float32)], 0)


def unpack_small(packed):
    row, lane = lane_masks()
    wide = jnp.where(row < 8, packed[0:1], packed[1:2])
    wide = jnp.where((row & 7) == (lane >> 4), wide, 0.0)
    tile = jnp.where((lane & 15) == row, 1.0, 0.0)
    point = lax.dot_general(wide, tile, NT, precision=HIGHEST, preferred_element_type=jnp.float32)
    return point, packed[2:3, 0:C]


def gathered_sum(refs):
    own, one, two, three = (ref[...] for ref in refs)
    return (own + one) + (two + three)


def mix_kernel(own_ref, one_ref, two_ref, three_ref, weight_ref, coef_ref, mixed_ref):
    coef = gathered_sum((own_ref, one_ref, two_ref, three_ref))
    coef_ref[...] = coef
    for a in range(M // GZ):
        total = jnp.zeros((C, MODES), jnp.float32)
        for i in range(C):
            total = total + coef_ref[a * C + i : a * C + i + 1, :] * weight_ref[a, i]
        mixed_ref[a * C : (a + 1) * C, :] = total


def pieces():
    for owner in range(M // GZ * 8):
        yield owner, owner // 8, owner // 4 % 2 * SUB, owner // 2 % 2 * SUB, owner % 2 * LANES


def back_kernel(own_ref, one_ref, two_ref, three_ref, weight_ref, coef_ref, back_ref, send_ref):
    full = gathered_sum((own_ref, one_ref, two_ref, three_ref))
    small = full[OWNED : OWNED + SUB, 0:LANES]
    for owner, a, i, o, p in pieces():
        send_ref[owner, 0:SUB, :] = coef_ref[a * C + i : a * C + i + SUB, p : p + LANES]
        send_ref[owner, SUB : 2 * SUB, :] = full[a * C + o : a * C + o + SUB, p : p + LANES]
        send_ref[owner, 2 * SUB : 3 * SUB, :] = small
    for a in range(M // GZ):
        grad = full[a * C : (a + 1) * C]
        for i in range(C):
            back_ref[a * C + i : a * C + i + 1, :] = (weight_ref[a, i] * grad).sum(
                0, keepdims=True
            )


def outer_kernel(spec_norm, cell_norm, got_ref, copies_ref, point_ref, bias_ref):
    samples = got_ref.shape[0]

    def body(s, carry):
        *totals, small = carry
        coef = got_ref[s, 0:SUB, :]
        grad = got_ref[s, SUB : 2 * SUB, :]
        totals = [total + coef[i : i + 1] * grad for i, total in enumerate(totals)]
        return (*totals, small + got_ref[s, 2 * SUB : 3 * SUB, :])

    zero = jnp.zeros((SUB, LANES), jnp.float32)
    *totals, small = lax.fori_loop(0, samples, body, (zero,) * (SUB + 1), unroll=8)
    for i, total in enumerate(totals):
        scaled = total * spec_norm
        for k in range(samples):
            copies_ref[k, i] = scaled
    point, sums = unpack_small(small)
    point_ref[...] = point * cell_norm
    bias_ref[...] = sums * cell_norm


def place_kernel(got_ref, out_ref):
    for owner, a, i, o, p in pieces():
        out_ref[a, i : i + SUB, o : o + SUB, p : p + LANES] = got_ref[owner]


def field_grad_kernel(
    sub_width,
    slab_ref,
    dpre_hbm,
    outer,
    inner,
    high,
    low,
    weight_ref,
    own_ref,
    one_ref,
    two_ref,
    three_ref,
    out_hbm,
    up,
    back,
    dpre,
    out,
    lines,
    kron_t,
    dpre_sems,
    out_sems,
):
    fetch = copies_in(dpre_hbm, dpre, dpre_sems)
    store = copies_out(out, out_hbm, out_sems)
    for step in range(CHUNKS):
        fetch(step).start()
    up[...] = spread(weight_ref[...])
    for k, ref in enumerate((own_ref, one_ref, two_ref, three_ref)):
        back[pl.ds(pl.multiple_of((slab_ref[0] ^ k) * OWNED, OWNED), OWNED), :] = ref[...]
    full = product((high[...], low[...]), split(back[...]), TN)
    lines[...] = (scale_fwd * full).reshape(C, ROWS, MODES).astype(bf16)

    for step in range(CHUNKS):
        kron_t[...] = kron_rows(outer, inner, step).T
        fetch(step).wait()
        for s in range(WIDTH // sub_width):
            cols = slice(step * WIDTH + s * sub_width, step * WIDTH + (s + 1) * sub_width)
            table = kron_t[:, s * sub_width : (s + 1) * sub_width]
            for x in range(ROWS // SUB):
                rows = slice(x * SUB, (x + 1) * SUB)
                values = dpre[:, rows, cols].reshape(C * SUB, sub_width)
                left = jnp.concatenate([lines[:, rows, :].reshape(C * SUB, MODES), up[...]], 1)
                grad = matmul(left, jnp.concatenate([table, values], 0))
                out[:, rows, cols] = grad.astype(bf16).reshape(C, SUB, sub_width)
        store(step).start()
    for step in range(CHUNKS):
        store(step).wait()


def shaped(*shape, dtype=jnp.float32):
    return jax.ShapeDtypeStruct(shape, dtype)


def limit(mebibytes):
    return pltpu.CompilerParams(vmem_limit_bytes=mebibytes << 20)


VM = pl.BlockSpec(memory_space=pltpu.VMEM)
SM = pl.BlockSpec(memory_space=pltpu.SMEM)
ANY = pl.BlockSpec(memory_space=pl.ANY)


def shards(field, cotangent, spec_weight, point_weight, bias):
    dp = lax.axis_size("dp")
    slab = lax.axis_index("gz").astype(jnp.int32).reshape(1)

    def exchange(parts):
        got = [parts[0]]
        for k in range(1, GZ):
            got.append(lax.ppermute(parts[k], "gz", [(g, g ^ k) for g in range(GZ)]))
        return got

    *coef_parts, outer, inner, high, low = pl.pallas_call(
        field_modes_kernel,
        out_shape=tuple(shaped(OWNED, MODES) for _ in range(GZ))
        + (
            shaped(N, MODES),
            shaped(N, MODES),
            shaped(M * C, C * ROWS, dtype=bf16),
            shaped(M * C, C * ROWS, dtype=bf16),
        ),
        in_specs=[SM, ANY],
        out_specs=(VM,) * (GZ + 4),
        scratch_shapes=[
            pltpu.VMEM((C, ROWS, CELLS), bf16),
            pltpu.VMEM((C * ROWS, MODES), jnp.float32),
            pltpu.SemaphoreType.DMA((CHUNKS,)),
        ],
        compiler_params=limit(53),
        name="field_modes",
    )(slab, field)

    coef, mixed = pl.pallas_call(
        mix_kernel,
        out_shape=(shaped(OWNED, MODES), shaped(OWNED, MODES)),
        compiler_params=limit(8),
        name="mix_modes",
    )(*exchange(coef_parts), spec_weight)
    mixed_all = lax.all_gather(mixed, "gz", axis=0, tiled=True)

    dpre, *grad_parts = pl.pallas_call(
        functools.partial(slope_kernel, 768),
        out_shape=(jax.ShapeDtypeStruct(field.shape, bf16),)
        + tuple(shaped(OWNED + SUB, MODES) for _ in range(GZ)),
        in_specs=[SM, ANY, ANY] + [VM] * 7,
        out_specs=(ANY,) + (VM,) * GZ,
        scratch_shapes=[
            pltpu.VMEM((C * SUB, C * SUB), bf16),
            pltpu.VMEM((C * SUB, C), bf16),
            pltpu.VMEM((C, ROWS, CELLS), bf16),
            pltpu.VMEM((C, ROWS, CELLS), bf16),
            pltpu.VMEM((C, ROWS, CELLS), bf16),
            pltpu.VMEM((C, ROWS, MODES), bf16),
            pltpu.VMEM((C * ROWS, MODES), jnp.float32),
            pltpu.VMEM((C * SUB, C * SUB), jnp.float32),
            pltpu.VMEM((WIDTH, MODES), bf16),
            pltpu.VMEM((MODES, WIDTH), bf16),
            pltpu.SemaphoreType.DMA((CHUNKS,)),
            pltpu.SemaphoreType.DMA((CHUNKS,)),
            pltpu.SemaphoreType.DMA((CHUNKS,)),
        ],
        compiler_params=limit(53),
        name="slope_and_modes",
    )(
        slab,
        field,
        cotangent,
        outer,
        inner,
        high,
        low,
        point_weight,
        bias.reshape(C, 1),
        mixed_all,
    )

    back, send = pl.pallas_call(
        back_kernel,
        out_shape=(shaped(OWNED, MODES), shaped(dp, 3 * SUB, LANES)),
        compiler_params=limit(8),
        name="back_modes",
    )(*exchange(grad_parts), spec_weight, coef)

    got = lax.all_to_all(send, "dp", 0, 0, tiled=True)
    back_parts = exchange([back] * GZ)
    copies, point_grad, bias_grad = pl.pallas_call(
        functools.partial(
            outer_kernel, 1.0 / math.sqrt(dp * N), 1.0 / math.sqrt(dp * N * N * N)
        ),
        out_shape=(shaped(dp, SUB, SUB, LANES), shaped(C, C), shaped(1, C)),
        compiler_params=limit(8),
        name="sample_sum",
    )(got)
    copies, *back_parts = lax.optimization_barrier((copies, *back_parts))
    owned = lax.all_to_all(copies, "dp", 0, 0, tiled=True)

    field_grad = pl.pallas_call(
        functools.partial(field_grad_kernel, 768),
        out_shape=jax.ShapeDtypeStruct(field.shape, bf16),
        in_specs=[SM, ANY] + [VM] * 9,
        out_specs=ANY,
        scratch_shapes=[
            pltpu.VMEM((C * SUB, C * SUB), bf16),
            pltpu.VMEM((M * C, MODES), jnp.float32),
            pltpu.VMEM((C, ROWS, CELLS), bf16),
            pltpu.VMEM((C, ROWS, CELLS), bf16),
            pltpu.VMEM((C, ROWS, MODES), bf16),
            pltpu.VMEM((MODES, WIDTH), bf16),
            pltpu.SemaphoreType.DMA((CHUNKS,)),
            pltpu.SemaphoreType.DMA((CHUNKS,)),
        ],
        compiler_params=limit(54),
        cost_estimate=pl.CostEstimate(
            flops=2 * C * ROWS * CELLS * (MODES + C * SUB),
            bytes_accessed=2 * C * ROWS * CELLS * 2,
            transcendentals=0,
        ),
        name="field_grad",
    )(slab, dpre, outer, inner, high, low, point_weight, *back_parts)

    spec_grad = pl.pallas_call(
        place_kernel,
        out_shape=shaped(M // GZ, C, C, MODES),
        compiler_params=limit(8),
        name="place_pieces",
    )(owned)
    return field_grad, spec_grad, point_grad, bias_grad.reshape(C)


def solution(mesh):
    return jax.shard_map(
        shards,
        mesh=mesh,
        in_specs=(
            P("dp", None, "gz", None),
            P("dp", None, "gz", None),
            P("gz", None, None, None),
            P(),
            P(),
        ),
        out_specs=(P("dp", None, "gz", None), P("gz", None, None, None), P(), P()),
        check_vma=False,
    )
```

```python
import functools
import math

import jax
import jax.numpy as jnp
from jax import lax
from jax.experimental import pallas as pl
from jax.experimental.pallas import tpu as pltpu
from jax.sharding import PartitionSpec as P

N = 96
M = 16
C = 16
GZ = 4
ROWS = N // GZ
CELLS = N * N
MODES = M * M
OWNED = M // GZ * C
SUB = 8
LANES = 128
CHUNKS = 6
WIDTH = CELLS // CHUNKS

bf16 = jnp.bfloat16
root_half = 0.7071067811865476
density_norm = 0.3989422804014327
scale_fwd = (2.0 / N) ** 1.5
scale_inv = (2.0 / M) ** 1.5
HIGHEST = lax.Precision.HIGHEST
NN = (((1,), (0,)), ((), ()))
NT = (((1,), (1,)), ((), ()))
TN = (((0,), (0,)), ((), ()))


def gelu_slope(values):
    cumulative = 0.5 * (1.0 + lax.erf(values * root_half))
    return cumulative + values * jnp.exp(-0.5 * values * values) * density_norm


def matmul(a, b, dims=NN):
    return lax.dot_general(a, b, dims, preferred_element_type=jnp.float32)


def split(values):
    high = values.astype(bf16)
    return high, (values - high.astype(jnp.float32)).astype(bf16)


def product(a, b, dims):
    return matmul(a[0], b[0], dims) + (matmul(a[0], b[1], dims) + matmul(a[1], b[0], dims))


def iota(shape, dim):
    return lax.broadcasted_iota(jnp.int32, shape, dim)


def quotient(values, divisor):
    return jnp.floor((values + 0.5) * (1.0 / divisor))


def basis_at(mode, position):
    cosine = mode < M // 2
    frequency = jnp.where(cosine, mode, mode - (M // 2 - 1))
    turns = frequency * position + jnp.where(cosine, 0.0, 0.75 * N)
    turns = turns - N * quotient(turns, N)
    return jnp.cos(turns * (2.0 * math.pi / N))


def cell_tables():
    mode = iota((N, MODES), 1)
    cell = iota((N, MODES), 0).astype(jnp.float32)
    outer = basis_at((mode >> 4).astype(jnp.float32), cell)
    return outer, basis_at((mode & 15).astype(jnp.float32), cell)


def row_matrix(slab):
    col = iota((M, C * ROWS), 1).astype(jnp.float32)
    x = col - ROWS * quotient(col, ROWS) + (slab * ROWS).astype(jnp.float32)
    table = basis_at(iota((M, C * ROWS), 0).astype(jnp.float32), x)
    wide = jnp.broadcast_to(table[:, None, :], (M, C, C * ROWS)).reshape(M * C, C * ROWS)
    row_channel = (iota((M * C, C * ROWS), 0) & 15).astype(jnp.float32)
    col_channel = quotient(iota((M * C, C * ROWS), 1).astype(jnp.float32), ROWS)
    return jnp.where(row_channel == col_channel, wide, 0.0)


def one_hot_rows(dtype):
    hit = (iota((C * SUB, C), 0) >> 3) == iota((C * SUB, C), 1)
    return jnp.where(hit, 1.0, 0.0).astype(dtype)


def same_sub():
    return (iota((C * SUB, C * SUB), 0) & 7) == (iota((C * SUB, C * SUB), 1) & 7)


def spread(weight):
    hot = one_hot_rows(bf16)
    tall = matmul(hot, weight).astype(bf16)
    return jnp.where(same_sub(), matmul(tall, hot, NT), 0.0).astype(bf16)


def send_parts(slab, high_ref, low_ref, acc, scale, refs):
    pair = split(acc)
    for k in range(GZ):
        first = pl.multiple_of((slab ^ k) * OWNED, OWNED)
        rows = (high_ref[pl.ds(first, OWNED), :], low_ref[pl.ds(first, OWNED), :])
        refs[k][0:OWNED, :] = scale * product(rows, pair, NN)


def chunk(step):
    if isinstance(step, int):
        return slice(step * WIDTH, (step + 1) * WIDTH)
    return pl.ds(pl.multiple_of(step * WIDTH, LANES), WIDTH)


def copies_in(source, target, sems):
    def copy(step):
        cols = chunk(step)
        return pltpu.make_async_copy(
            source.at[0, :, :, cols], target.at[:, :, cols], sems.at[step]
        )

    return copy


def copies_out(source, target, sems):
    def copy(step):
        cols = chunk(step)
        return pltpu.make_async_copy(
            source.at[:, :, cols], target.at[0, :, :, cols], sems.at[step]
        )

    return copy


def kron_rows(outer, inner, step):
    table = inner[...]
    rows = [
        (outer[pl.ds(step * (WIDTH // N) + k, 1), :] * table).astype(bf16)
        for k in range(WIDTH // N)
    ]
    return jnp.concatenate(rows, 0)


def field_modes_kernel(slab_ref, field_hbm, *rest):
    parts = rest[:GZ]
    outer, inner, high, low, field, acc, sems = rest[GZ:]
    fetch = copies_in(field_hbm, field, sems)
    for step in range(CHUNKS):
        fetch(step).start()
    outer[...], inner[...] = cell_tables()
    high[...], low[...] = split(row_matrix(slab_ref[0]))
    acc[...] = jnp.zeros_like(acc)

    def body(step, carry):
        kron = kron_rows(outer, inner, step)
        fetch(step).wait()
        acc[...] += matmul(field[:, :, chunk(step)].reshape(C * ROWS, WIDTH), kron)
        return carry

    lax.fori_loop(0, CHUNKS, body, 0)
    send_parts(slab_ref[0], high, low, acc[...], scale_fwd, parts)


def slope_kernel(
    sub_width,
    slab_ref,
    field_hbm,
    cot_hbm,
    outer,
    inner,
    high,
    low,
    weight_ref,
    bias_ref,
    mixed_ref,
    dpre_hbm,
    *rest,
):
    parts = rest[:GZ]
    down, bias_cols, field, cot, out, lines, acc, point_acc, kron, kron_t, *sems = rest[GZ:]
    field_sems, cot_sems, out_sems = sems
    fetch_field = copies_in(field_hbm, field, field_sems)
    fetch_cot = copies_in(cot_hbm, cot, cot_sems)
    store = copies_out(out, dpre_hbm, out_sems)
    for step in range(CHUNKS):
        fetch_field(step).start()
        fetch_cot(step).start()
    down[...] = spread(weight_ref[...].T)
    bias_high, bias_low = split(
        jnp.dot(
            one_hot_rows(jnp.float32),
            bias_ref[...],
            precision=HIGHEST,
            preferred_element_type=jnp.float32,
        )
    )
    lane = iota((C * SUB, C), 1)
    bias_cols[...] = jnp.where(
        lane == 0,
        bias_high.astype(jnp.float32),
        jnp.where(lane == 1, bias_low.astype(jnp.float32), 0.0),
    ).astype(bf16)
    ones = jnp.ones((C, sub_width), bf16)
    full = product((high[...], low[...]), split(mixed_ref[...]), TN)
    lines[...] = (scale_inv * full).reshape(C, ROWS, MODES).astype(bf16)
    acc[...] = jnp.zeros_like(acc)
    point_acc[...] = jnp.zeros_like(point_acc)

    for step in range(CHUNKS):
        kron[...] = kron_rows(outer, inner, step)
        kron_t[...] = kron[...].T
        fetch_field(step).wait()
        fetch_cot(step).wait()
        for s in range(WIDTH // sub_width):
            cols = slice(step * WIDTH + s * sub_width, step * WIDTH + (s + 1) * sub_width)
            table = kron_t[:, s * sub_width : (s + 1) * sub_width]
            for x in range(ROWS // SUB):
                rows = slice(x * SUB, (x + 1) * SUB)
                values = field[:, rows, cols].reshape(C * SUB, sub_width)
                left = jnp.concatenate(
                    [lines[:, rows, :].reshape(C * SUB, MODES), down[...], bias_cols[...]], 1
                )
                pre = matmul(left, jnp.concatenate([table, values, ones], 0))
                grad = cot[:, rows, cols].reshape(C * SUB, sub_width).astype(jnp.float32)
                dpre = (grad * gelu_slope(pre)).astype(bf16)
                out[:, rows, cols] = dpre.reshape(C, SUB, sub_width)
        store(step).start()
        cols = chunk(step)
        for x in range(ROWS // SUB):
            rows = slice(x * SUB, (x + 1) * SUB)
            point_acc[...] += matmul(
                field[:, rows, cols].reshape(C * SUB, WIDTH),
                out[:, rows, cols].reshape(C * SUB, WIDTH),
                NT,
            )
        acc[...] += matmul(out[:, :, cols].reshape(C * ROWS, WIDTH), kron[...])
    send_parts(slab_ref[0], high, low, acc[...], scale_inv, parts)
    sums = acc[:, 0:LANES].reshape(C, ROWS, LANES).sum(1)[:, 0:1]
    packed = pack_small(point_acc[...], sums)
    for k in range(GZ):
        parts[k][OWNED : OWNED + SUB, 0:LANES] = packed
        parts[k][OWNED : OWNED + SUB, LANES:MODES] = jnp.zeros_like(packed)
    for step in range(CHUNKS):
        store(step).wait()


def lane_masks():
    return iota((C, LANES), 0), iota((C, LANES), 1)


def pack_small(blocks, sums):
    fold = jnp.where((iota((C * SUB, LANES), 0) >> 3) == (iota((C * SUB, LANES), 1) & 15), 1.0, 0.0)
    fold = fold.astype(bf16)
    high, low = split(jnp.where(same_sub(), blocks, 0.0))
    wide = matmul(high, fold) + matmul(low, fold)
    channel = (iota((C * SUB, LANES), 0) >> 3) & 7
    wide = jnp.where(channel == (iota((C * SUB, LANES), 1) >> 4), wide, 0.0)
    first = wide[0 : 8 * SUB].sum(0, keepdims=True)
    second = wide[8 * SUB :].sum(0, keepdims=True)
    row, lane = lane_masks()
    vector = jnp.where(row == lane, sums, 0.0).sum(0, keepdims=True)
    return jnp.concatenate([first, second, vector, jnp.zeros((5, LANES), jnp.float32)], 0)


def unpack_small(packed):
    row, lane = lane_masks()
    wide = jnp.where(row < 8, packed[0:1], packed[1:2])
    wide = jnp.where((row & 7) == (lane >> 4), wide, 0.0)
    tile = jnp.where((lane & 15) == row, 1.0, 0.0)
    point = lax.dot_general(wide, tile, NT, precision=HIGHEST, preferred_element_type=jnp.float32)
    return point, packed[2:3, 0:C]


def add_kernel(a_ref, b_ref, out_ref):
    out_ref[...] = a_ref[...] + b_ref[...]


def mix_kernel(own_ref, one_ref, two_ref, weight_ref, coef_ref, mixed_ref):
    coef_ref[...] = (own_ref[...] + one_ref[...]) + two_ref[...]
    for a in range(M // GZ):
        total = jnp.zeros((C, MODES), jnp.float32)
        for i in range(C):
            total = total + coef_ref[a * C + i : a * C + i + 1, :] * weight_ref[a, i]
        mixed_ref[a * C : (a + 1) * C, :] = total


def pieces():
    for owner in range(M // GZ * 8):
        yield owner, owner // 8, owner // 4 % 2 * SUB, owner // 2 % 2 * SUB, owner % 2 * LANES


def back_kernel(own_ref, one_ref, two_ref, weight_ref, coef_ref, back_ref, send_ref):
    full = (own_ref[...] + one_ref[...]) + two_ref[...]
    small = full[OWNED : OWNED + SUB, 0:LANES]
    for owner, a, i, o, p in pieces():
        send_ref[owner, 0:SUB, :] = coef_ref[a * C + i : a * C + i + SUB, p : p + LANES]
        send_ref[owner, SUB : 2 * SUB, :] = full[a * C + o : a * C + o + SUB, p : p + LANES]
        send_ref[owner, 2 * SUB : 3 * SUB, :] = small
    for a in range(M // GZ):
        grad = full[a * C : (a + 1) * C]
        for i in range(C):
            back_ref[a * C + i : a * C + i + 1, :] = (weight_ref[a, i] * grad).sum(
                0, keepdims=True
            )


def outer_kernel(spec_norm, cell_norm, got_ref, copies_ref, point_ref, bias_ref):
    samples = got_ref.shape[0]

    def body(s, carry):
        *totals, small = carry
        coef = got_ref[s, 0:SUB, :]
        grad = got_ref[s, SUB : 2 * SUB, :]
        totals = [total + coef[i : i + 1] * grad for i, total in enumerate(totals)]
        return (*totals, small + got_ref[s, 2 * SUB : 3 * SUB, :])

    zero = jnp.zeros((SUB, LANES), jnp.float32)
    *totals, small = lax.fori_loop(0, samples, body, (zero,) * (SUB + 1), unroll=8)
    for i, total in enumerate(totals):
        scaled = total * spec_norm
        for k in range(samples):
            copies_ref[k, i] = scaled
    point, sums = unpack_small(small)
    point_ref[...] = point * cell_norm
    bias_ref[...] = sums * cell_norm


def place_kernel(got_ref, out_ref):
    for owner, a, i, o, p in pieces():
        out_ref[a, i : i + SUB, o : o + SUB, p : p + LANES] = got_ref[owner]


def field_grad_kernel(
    sub_width,
    slab_ref,
    dpre_hbm,
    outer,
    inner,
    high,
    low,
    weight_ref,
    own_ref,
    one_ref,
    two_ref,
    three_ref,
    out_hbm,
    up,
    back,
    dpre,
    out,
    lines,
    kron_t,
    dpre_sems,
    out_sems,
):
    fetch = copies_in(dpre_hbm, dpre, dpre_sems)
    store = copies_out(out, out_hbm, out_sems)
    for step in range(CHUNKS):
        fetch(step).start()
    up[...] = spread(weight_ref[...])
    for k, ref in enumerate((own_ref, one_ref, two_ref, three_ref)):
        back[pl.ds(pl.multiple_of((slab_ref[0] ^ k) * OWNED, OWNED), OWNED), :] = ref[...]
    full = product((high[...], low[...]), split(back[...]), TN)
    lines[...] = (scale_fwd * full).reshape(C, ROWS, MODES).astype(bf16)

    for step in range(CHUNKS):
        kron_t[...] = kron_rows(outer, inner, step).T
        fetch(step).wait()
        for s in range(WIDTH // sub_width):
            cols = slice(step * WIDTH + s * sub_width, step * WIDTH + (s + 1) * sub_width)
            table = kron_t[:, s * sub_width : (s + 1) * sub_width]
            for x in range(ROWS // SUB):
                rows = slice(x * SUB, (x + 1) * SUB)
                values = dpre[:, rows, cols].reshape(C * SUB, sub_width)
                left = jnp.concatenate([lines[:, rows, :].reshape(C * SUB, MODES), up[...]], 1)
                grad = matmul(left, jnp.concatenate([table, values], 0))
                out[:, rows, cols] = grad.astype(bf16).reshape(C, SUB, sub_width)
        store(step).start()
    for step in range(CHUNKS):
        store(step).wait()


def shaped(*shape, dtype=jnp.float32):
    return jax.ShapeDtypeStruct(shape, dtype)


def limit(mebibytes):
    return pltpu.CompilerParams(vmem_limit_bytes=mebibytes << 20)


VM = pl.BlockSpec(memory_space=pltpu.VMEM)
SM = pl.BlockSpec(memory_space=pltpu.SMEM)
ANY = pl.BlockSpec(memory_space=pl.ANY)


def shards(field, cotangent, spec_weight, point_weight, bias):
    dp = lax.axis_size("dp")
    slab = lax.axis_index("gz").astype(jnp.int32).reshape(1)

    def flip(values, k):
        return lax.ppermute(values, "gz", [(g, g ^ k) for g in range(GZ)])

    def reduce_parts(parts):
        three = flip(parts[3], 1)
        one = flip(parts[1], 1)
        forward = pl.pallas_call(
            add_kernel,
            out_shape=jax.ShapeDtypeStruct(three.shape, three.dtype),
            compiler_params=limit(8),
            name="add_pair",
        )(parts[2], three)
        return parts[0], one, flip(forward, 2)

    *coef_parts, outer, inner, high, low = pl.pallas_call(
        field_modes_kernel,
        out_shape=tuple(shaped(OWNED, MODES) for _ in range(GZ))
        + (
            shaped(N, MODES),
            shaped(N, MODES),
            shaped(M * C, C * ROWS, dtype=bf16),
            shaped(M * C, C * ROWS, dtype=bf16),
        ),
        in_specs=[SM, ANY],
        out_specs=(VM,) * (GZ + 4),
        scratch_shapes=[
            pltpu.VMEM((C, ROWS, CELLS), bf16),
            pltpu.VMEM((C * ROWS, MODES), jnp.float32),
            pltpu.SemaphoreType.DMA((CHUNKS,)),
        ],
        compiler_params=limit(53),
        name="field_modes",
    )(slab, field)

    coef, mixed = pl.pallas_call(
        mix_kernel,
        out_shape=(shaped(OWNED, MODES), shaped(OWNED, MODES)),
        compiler_params=limit(8),
        name="mix_modes",
    )(*reduce_parts(coef_parts), spec_weight)
    mixed_all = lax.all_gather(mixed, "gz", axis=0, tiled=True)

    dpre, *grad_parts = pl.pallas_call(
        functools.partial(slope_kernel, 768),
        out_shape=(jax.ShapeDtypeStruct(field.shape, bf16),)
        + tuple(shaped(OWNED + SUB, MODES) for _ in range(GZ)),
        in_specs=[SM, ANY, ANY] + [VM] * 7,
        out_specs=(ANY,) + (VM,) * GZ,
        scratch_shapes=[
            pltpu.VMEM((C * SUB, C * SUB), bf16),
            pltpu.VMEM((C * SUB, C), bf16),
            pltpu.VMEM((C, ROWS, CELLS), bf16),
            pltpu.VMEM((C, ROWS, CELLS), bf16),
            pltpu.VMEM((C, ROWS, CELLS), bf16),
            pltpu.VMEM((C, ROWS, MODES), bf16),
            pltpu.VMEM((C * ROWS, MODES), jnp.float32),
            pltpu.VMEM((C * SUB, C * SUB), jnp.float32),
            pltpu.VMEM((WIDTH, MODES), bf16),
            pltpu.VMEM((MODES, WIDTH), bf16),
            pltpu.SemaphoreType.DMA((CHUNKS,)),
            pltpu.SemaphoreType.DMA((CHUNKS,)),
            pltpu.SemaphoreType.DMA((CHUNKS,)),
        ],
        compiler_params=limit(53),
        name="slope_and_modes",
    )(
        slab,
        field,
        cotangent,
        outer,
        inner,
        high,
        low,
        point_weight,
        bias.reshape(C, 1),
        mixed_all,
    )

    back, send = pl.pallas_call(
        back_kernel,
        out_shape=(shaped(OWNED, MODES), shaped(dp, 3 * SUB, LANES)),
        compiler_params=limit(8),
        name="back_modes",
    )(*reduce_parts(grad_parts), spec_weight, coef)

    got = lax.all_to_all(send, "dp", 0, 0, tiled=True)
    two = flip(back, 2)
    back_parts = (back, flip(back, 1), two, flip(two, 1))
    copies, point_grad, bias_grad = pl.pallas_call(
        functools.partial(
            outer_kernel, 1.0 / math.sqrt(dp * N), 1.0 / math.sqrt(dp * N * N * N)
        ),
        out_shape=(shaped(dp, SUB, SUB, LANES), shaped(C, C), shaped(1, C)),
        compiler_params=limit(8),
        name="sample_sum",
    )(got)
    copies, *back_parts = lax.optimization_barrier((copies, *back_parts))
    owned = lax.all_to_all(copies, "dp", 0, 0, tiled=True)

    field_grad = pl.pallas_call(
        functools.partial(field_grad_kernel, 768),
        out_shape=jax.ShapeDtypeStruct(field.shape, bf16),
        in_specs=[SM, ANY] + [VM] * 9,
        out_specs=ANY,
        scratch_shapes=[
            pltpu.VMEM((C * SUB, C * SUB), bf16),
            pltpu.VMEM((M * C, MODES), jnp.float32),
            pltpu.VMEM((C, ROWS, CELLS), bf16),
            pltpu.VMEM((C, ROWS, CELLS), bf16),
            pltpu.VMEM((C, ROWS, MODES), bf16),
            pltpu.VMEM((MODES, WIDTH), bf16),
            pltpu.SemaphoreType.DMA((CHUNKS,)),
            pltpu.SemaphoreType.DMA((CHUNKS,)),
        ],
        compiler_params=limit(54),
        cost_estimate=pl.CostEstimate(
            flops=2 * C * ROWS * CELLS * (MODES + C * SUB),
            bytes_accessed=2 * C * ROWS * CELLS * 2,
            transcendentals=0,
        ),
        name="field_grad",
    )(slab, dpre, outer, inner, high, low, point_weight, *back_parts)

    spec_grad = pl.pallas_call(
        place_kernel,
        out_shape=shaped(M // GZ, C, C, MODES),
        compiler_params=limit(8),
        name="place_pieces",
    )(owned)
    return field_grad, spec_grad, point_grad, bias_grad.reshape(C)


def solution(mesh):
    return jax.shard_map(
        shards,
        mesh=mesh,
        in_specs=(
            P("dp", None, "gz", None),
            P("dp", None, "gz", None),
            P("gz", None, None, None),
            P(),
            P(),
        ),
        out_specs=(P("dp", None, "gz", None), P("gz", None, None, None), P(), P()),
        check_vma=False,
    )
```

```python
import functools
import math

import jax
import jax.numpy as jnp
from jax import lax
from jax.experimental import pallas as pl
from jax.experimental.pallas import tpu as pltpu
from jax.sharding import PartitionSpec as P

N = 96
M = 16
C = 16
GZ = 4
ROWS = N // GZ
CELLS = N * N
MODES = M * M
OWNED = M // GZ * C
SUB = 8
LANES = 128
CHUNKS = 6
WIDTH = CELLS // CHUNKS

bf16 = jnp.bfloat16
root_half = 0.7071067811865476
density_norm = 0.3989422804014327
scale_fwd = (2.0 / N) ** 1.5
scale_inv = (2.0 / M) ** 1.5
HIGHEST = lax.Precision.HIGHEST
NN = (((1,), (0,)), ((), ()))
NT = (((1,), (1,)), ((), ()))
TN = (((0,), (0,)), ((), ()))


def gelu_slope(values):
    cumulative = 0.5 * (1.0 + lax.erf(values * root_half))
    return cumulative + values * jnp.exp(-0.5 * values * values) * density_norm


def matmul(a, b, dims=NN):
    return lax.dot_general(a, b, dims, preferred_element_type=jnp.float32)


def split(values):
    high = values.astype(bf16)
    return high, (values - high.astype(jnp.float32)).astype(bf16)


def product(a, b, dims):
    return matmul(a[0], b[0], dims) + (matmul(a[0], b[1], dims) + matmul(a[1], b[0], dims))


def iota(shape, dim):
    return lax.broadcasted_iota(jnp.int32, shape, dim)


def quotient(values, divisor):
    return jnp.floor((values + 0.5) * (1.0 / divisor))


def basis_at(mode, position):
    cosine = mode < M // 2
    frequency = jnp.where(cosine, mode, mode - (M // 2 - 1))
    turns = frequency * position + jnp.where(cosine, 0.0, 0.75 * N)
    turns = turns - N * quotient(turns, N)
    return jnp.cos(turns * (2.0 * math.pi / N))


def cell_tables():
    mode = iota((N, MODES), 1)
    cell = iota((N, MODES), 0).astype(jnp.float32)
    outer = basis_at((mode >> 4).astype(jnp.float32), cell)
    return outer, basis_at((mode & 15).astype(jnp.float32), cell)


def row_matrix(slab):
    col = iota((M, C * ROWS), 1).astype(jnp.float32)
    x = col - ROWS * quotient(col, ROWS) + (slab * ROWS).astype(jnp.float32)
    table = basis_at(iota((M, C * ROWS), 0).astype(jnp.float32), x)
    wide = jnp.broadcast_to(table[:, None, :], (M, C, C * ROWS)).reshape(M * C, C * ROWS)
    row_channel = (iota((M * C, C * ROWS), 0) & 15).astype(jnp.float32)
    col_channel = quotient(iota((M * C, C * ROWS), 1).astype(jnp.float32), ROWS)
    return jnp.where(row_channel == col_channel, wide, 0.0)


def one_hot_rows(dtype):
    hit = (iota((C * SUB, C), 0) >> 3) == iota((C * SUB, C), 1)
    return jnp.where(hit, 1.0, 0.0).astype(dtype)


def same_sub():
    return (iota((C * SUB, C * SUB), 0) & 7) == (iota((C * SUB, C * SUB), 1) & 7)


def spread(weight):
    hot = one_hot_rows(bf16)
    tall = matmul(hot, weight).astype(bf16)
    return jnp.where(same_sub(), matmul(tall, hot, NT), 0.0).astype(bf16)


def send_parts(slab, high_ref, low_ref, acc, scale, joined, refs):
    joined[...] = scale * product((high_ref[...], low_ref[...]), split(acc), NN)
    for k in range(GZ):
        first = pl.multiple_of((slab ^ k) * OWNED, OWNED)
        refs[k][0:OWNED, :] = joined[pl.ds(first, OWNED), :]


def chunk(step):
    if isinstance(step, int):
        return slice(step * WIDTH, (step + 1) * WIDTH)
    return pl.ds(pl.multiple_of(step * WIDTH, LANES), WIDTH)


def copies_in(source, target, sems):
    def copy(step):
        cols = chunk(step)
        return pltpu.make_async_copy(
            source.at[0, :, :, cols], target.at[:, :, cols], sems.at[step]
        )

    return copy


def copies_out(source, target, sems):
    def copy(step):
        cols = chunk(step)
        return pltpu.make_async_copy(
            source.at[:, :, cols], target.at[0, :, :, cols], sems.at[step]
        )

    return copy


def kron_rows(outer, inner, step):
    table = inner[...]
    rows = [
        (outer[pl.ds(step * (WIDTH // N) + k, 1), :] * table).astype(bf16)
        for k in range(WIDTH // N)
    ]
    return jnp.concatenate(rows, 0)


def field_modes_kernel(slab_ref, field_hbm, *rest):
    parts = rest[:GZ]
    outer, inner, high, low, field, acc, joined, sems = rest[GZ:]
    fetch = copies_in(field_hbm, field, sems)
    for step in range(CHUNKS):
        fetch(step).start()
    outer[...], inner[...] = cell_tables()
    high[...], low[...] = split(row_matrix(slab_ref[0]))
    acc[...] = jnp.zeros_like(acc)

    def body(step, carry):
        kron = kron_rows(outer, inner, step)
        fetch(step).wait()
        acc[...] += matmul(field[:, :, chunk(step)].reshape(C * ROWS, WIDTH), kron)
        return carry

    lax.fori_loop(0, CHUNKS, body, 0)
    send_parts(slab_ref[0], high, low, acc[...], scale_fwd, joined, parts)


def join_parts(slab, refs, joined):
    for k, ref in enumerate(refs):
        joined[pl.ds(pl.multiple_of((slab ^ k) * OWNED, OWNED), OWNED), :] = ref[...]


def slope_kernel(
    sub_width,
    slab_ref,
    field_hbm,
    cot_hbm,
    outer,
    inner,
    high,
    low,
    weight_ref,
    bias_ref,
    own_ref,
    one_ref,
    two_ref,
    three_ref,
    dpre_hbm,
    *rest,
):
    parts = rest[:GZ]
    mixed, down, bias_cols, field, cot, out, lines, acc, point_acc, kron, kron_t, *sems = rest[GZ:]
    field_sems, cot_sems, out_sems = sems
    fetch_field = copies_in(field_hbm, field, field_sems)
    fetch_cot = copies_in(cot_hbm, cot, cot_sems)
    store = copies_out(out, dpre_hbm, out_sems)
    for step in range(CHUNKS):
        fetch_field(step).start()
        fetch_cot(step).start()
    down[...] = spread(weight_ref[...].T)
    bias_high, bias_low = split(
        jnp.dot(
            one_hot_rows(jnp.float32),
            bias_ref[...],
            precision=HIGHEST,
            preferred_element_type=jnp.float32,
        )
    )
    lane = iota((C * SUB, C), 1)
    bias_cols[...] = jnp.where(
        lane == 0,
        bias_high.astype(jnp.float32),
        jnp.where(lane == 1, bias_low.astype(jnp.float32), 0.0),
    ).astype(bf16)
    ones = jnp.ones((C, sub_width), bf16)
    join_parts(slab_ref[0], (own_ref, one_ref, two_ref, three_ref), mixed)
    full = product((high[...], low[...]), split(mixed[...]), TN)
    lines[...] = (scale_inv * full).reshape(C, ROWS, MODES).astype(bf16)
    acc[...] = jnp.zeros_like(acc)
    point_acc[...] = jnp.zeros_like(point_acc)

    for step in range(CHUNKS):
        kron[...] = kron_rows(outer, inner, step)
        kron_t[...] = kron[...].T
        fetch_field(step).wait()
        fetch_cot(step).wait()
        for s in range(WIDTH // sub_width):
            cols = slice(step * WIDTH + s * sub_width, step * WIDTH + (s + 1) * sub_width)
            table = kron_t[:, s * sub_width : (s + 1) * sub_width]
            for x in range(ROWS // SUB):
                rows = slice(x * SUB, (x + 1) * SUB)
                values = field[:, rows, cols].reshape(C * SUB, sub_width)
                left = jnp.concatenate(
                    [lines[:, rows, :].reshape(C * SUB, MODES), down[...], bias_cols[...]], 1
                )
                pre = matmul(left, jnp.concatenate([table, values, ones], 0))
                grad = cot[:, rows, cols].reshape(C * SUB, sub_width).astype(jnp.float32)
                dpre = (grad * gelu_slope(pre)).astype(bf16)
                out[:, rows, cols] = dpre.reshape(C, SUB, sub_width)
        store(step).start()
        cols = chunk(step)
        for x in range(ROWS // SUB):
            rows = slice(x * SUB, (x + 1) * SUB)
            point_acc[...] += matmul(
                field[:, rows, cols].reshape(C * SUB, WIDTH),
                out[:, rows, cols].reshape(C * SUB, WIDTH),
                NT,
            )
        acc[...] += matmul(out[:, :, cols].reshape(C * ROWS, WIDTH), kron[...])
    send_parts(slab_ref[0], high, low, acc[...], scale_inv, mixed, parts)
    sums = acc[:, 0:LANES].reshape(C, ROWS, LANES).sum(1)[:, 0:1]
    packed = pack_small(point_acc[...], sums)
    for k in range(GZ):
        parts[k][OWNED : OWNED + SUB, 0:LANES] = packed
        parts[k][OWNED : OWNED + SUB, LANES:MODES] = jnp.zeros_like(packed)
    for step in range(CHUNKS):
        store(step).wait()


def lane_masks():
    return iota((C, LANES), 0), iota((C, LANES), 1)


def pack_small(blocks, sums):
    fold = jnp.where((iota((C * SUB, LANES), 0) >> 3) == (iota((C * SUB, LANES), 1) & 15), 1.0, 0.0)
    fold = fold.astype(bf16)
    high, low = split(jnp.where(same_sub(), blocks, 0.0))
    wide = matmul(high, fold) + matmul(low, fold)
    channel = (iota((C * SUB, LANES), 0) >> 3) & 7
    wide = jnp.where(channel == (iota((C * SUB, LANES), 1) >> 4), wide, 0.0)
    first = wide[0 : 8 * SUB].sum(0, keepdims=True)
    second = wide[8 * SUB :].sum(0, keepdims=True)
    row, lane = lane_masks()
    vector = jnp.where(row == lane, sums, 0.0).sum(0, keepdims=True)
    return jnp.concatenate([first, second, vector, jnp.zeros((5, LANES), jnp.float32)], 0)


def unpack_small(packed):
    row, lane = lane_masks()
    wide = jnp.where(row < 8, packed[0:1], packed[1:2])
    wide = jnp.where((row & 7) == (lane >> 4), wide, 0.0)
    tile = jnp.where((lane & 15) == row, 1.0, 0.0)
    point = lax.dot_general(wide, tile, NT, precision=HIGHEST, preferred_element_type=jnp.float32)
    return point, packed[2:3, 0:C]


def add_kernel(a_ref, b_ref, out_ref):
    out_ref[...] = a_ref[...] + b_ref[...]


def mix_kernel(own_ref, one_ref, two_ref, weight_ref, coef_ref, mixed_ref):
    coef_ref[...] = (own_ref[...] + one_ref[...]) + two_ref[...]
    for a in range(M // GZ):
        total = jnp.zeros((C, MODES), jnp.float32)
        for i in range(C):
            total = total + coef_ref[a * C + i : a * C + i + 1, :] * weight_ref[a, i]
        mixed_ref[a * C : (a + 1) * C, :] = total


def pieces():
    for owner in range(M // GZ * 8):
        yield owner, owner // 8, owner // 4 % 2 * SUB, owner // 2 % 2 * SUB, owner % 2 * LANES


def back_kernel(own_ref, one_ref, two_ref, weight_ref, coef_ref, back_ref, send_ref):
    full = (own_ref[...] + one_ref[...]) + two_ref[...]
    small = full[OWNED : OWNED + SUB, 0:LANES]
    for owner, a, i, o, p in pieces():
        send_ref[owner, 0:SUB, :] = coef_ref[a * C + i : a * C + i + SUB, p : p + LANES]
        send_ref[owner, SUB : 2 * SUB, :] = full[a * C + o : a * C + o + SUB, p : p + LANES]
        send_ref[owner, 2 * SUB : 3 * SUB, :] = small
    for a in range(M // GZ):
        grad = full[a * C : (a + 1) * C]
        for i in range(C):
            back_ref[a * C + i : a * C + i + 1, :] = (weight_ref[a, i] * grad).sum(
                0, keepdims=True
            )


def outer_kernel(spec_norm, cell_norm, got_ref, copies_ref, point_ref, bias_ref):
    samples = got_ref.shape[0]

    def body(s, carry):
        *totals, small = carry
        coef = got_ref[s, 0:SUB, :]
        grad = got_ref[s, SUB : 2 * SUB, :]
        totals = [total + coef[i : i + 1] * grad for i, total in enumerate(totals)]
        return (*totals, small + got_ref[s, 2 * SUB : 3 * SUB, :])

    zero = jnp.zeros((SUB, LANES), jnp.float32)
    *totals, small = lax.fori_loop(0, samples, body, (zero,) * (SUB + 1), unroll=8)
    for i, total in enumerate(totals):
        scaled = total * spec_norm
        for k in range(samples):
            copies_ref[k, i] = scaled
    point, sums = unpack_small(small)
    point_ref[...] = point * cell_norm
    bias_ref[...] = sums * cell_norm


def place_kernel(got_ref, out_ref):
    for owner, a, i, o, p in pieces():
        out_ref[a, i : i + SUB, o : o + SUB, p : p + LANES] = got_ref[owner]


def field_grad_kernel(
    sub_width,
    slab_ref,
    dpre_hbm,
    outer,
    inner,
    high,
    low,
    weight_ref,
    own_ref,
    one_ref,
    two_ref,
    three_ref,
    out_hbm,
    up,
    back,
    dpre,
    out,
    lines,
    kron_t,
    dpre_sems,
    out_sems,
):
    fetch = copies_in(dpre_hbm, dpre, dpre_sems)
    store = copies_out(out, out_hbm, out_sems)
    for step in range(CHUNKS):
        fetch(step).start()
    up[...] = spread(weight_ref[...])
    join_parts(slab_ref[0], (own_ref, one_ref, two_ref, three_ref), back)
    full = product((high[...], low[...]), split(back[...]), TN)
    lines[...] = (scale_fwd * full).reshape(C, ROWS, MODES).astype(bf16)

    for step in range(CHUNKS):
        kron_t[...] = kron_rows(outer, inner, step).T
        fetch(step).wait()
        for s in range(WIDTH // sub_width):
            cols = slice(step * WIDTH + s * sub_width, step * WIDTH + (s + 1) * sub_width)
            table = kron_t[:, s * sub_width : (s + 1) * sub_width]
            for x in range(ROWS // SUB):
                rows = slice(x * SUB, (x + 1) * SUB)
                values = dpre[:, rows, cols].reshape(C * SUB, sub_width)
                left = jnp.concatenate([lines[:, rows, :].reshape(C * SUB, MODES), up[...]], 1)
                grad = matmul(left, jnp.concatenate([table, values], 0))
                out[:, rows, cols] = grad.astype(bf16).reshape(C, SUB, sub_width)
        store(step).start()
    for step in range(CHUNKS):
        store(step).wait()


def shaped(*shape, dtype=jnp.float32):
    return jax.ShapeDtypeStruct(shape, dtype)


def limit(mebibytes):
    return pltpu.CompilerParams(vmem_limit_bytes=mebibytes << 20)


VM = pl.BlockSpec(memory_space=pltpu.VMEM)
SM = pl.BlockSpec(memory_space=pltpu.SMEM)
ANY = pl.BlockSpec(memory_space=pl.ANY)


def shards(field, cotangent, spec_weight, point_weight, bias):
    dp = lax.axis_size("dp")
    slab = lax.axis_index("gz").astype(jnp.int32).reshape(1)

    def flip(values, k):
        return lax.ppermute(values, "gz", [(g, g ^ k) for g in range(GZ)])

    def reduce_parts(parts):
        three = flip(parts[3], 1)
        one = flip(parts[1], 1)
        forward = pl.pallas_call(
            add_kernel,
            out_shape=jax.ShapeDtypeStruct(three.shape, three.dtype),
            compiler_params=limit(8),
            name="add_pair",
        )(parts[2], three)
        return parts[0], one, flip(forward, 2)

    *coef_parts, outer, inner, high, low = pl.pallas_call(
        field_modes_kernel,
        out_shape=tuple(shaped(OWNED, MODES) for _ in range(GZ))
        + (
            shaped(N, MODES),
            shaped(N, MODES),
            shaped(M * C, C * ROWS, dtype=bf16),
            shaped(M * C, C * ROWS, dtype=bf16),
        ),
        in_specs=[SM, ANY],
        out_specs=(VM,) * (GZ + 4),
        scratch_shapes=[
            pltpu.VMEM((C, ROWS, CELLS), bf16),
            pltpu.VMEM((C * ROWS, MODES), jnp.float32),
            pltpu.VMEM((M * C, MODES), jnp.float32),
            pltpu.SemaphoreType.DMA((CHUNKS,)),
        ],
        compiler_params=limit(53),
        name="field_modes",
    )(slab, field)

    coef, mixed = pl.pallas_call(
        mix_kernel,
        out_shape=(shaped(OWNED, MODES), shaped(OWNED, MODES)),
        compiler_params=limit(8),
        name="mix_modes",
    )(*reduce_parts(coef_parts), spec_weight)
    mixed_two = flip(mixed, 2)
    mixed_parts = (mixed, flip(mixed, 1), mixed_two, flip(mixed_two, 1))

    dpre, *grad_parts = pl.pallas_call(
        functools.partial(slope_kernel, 768),
        out_shape=(jax.ShapeDtypeStruct(field.shape, bf16),)
        + tuple(shaped(OWNED + SUB, MODES) for _ in range(GZ)),
        in_specs=[SM, ANY, ANY] + [VM] * 10,
        out_specs=(ANY,) + (VM,) * GZ,
        scratch_shapes=[
            pltpu.VMEM((M * C, MODES), jnp.float32),
            pltpu.VMEM((C * SUB, C * SUB), bf16),
            pltpu.VMEM((C * SUB, C), bf16),
            pltpu.VMEM((C, ROWS, CELLS), bf16),
            pltpu.VMEM((C, ROWS, CELLS), bf16),
            pltpu.VMEM((C, ROWS, CELLS), bf16),
            pltpu.VMEM((C, ROWS, MODES), bf16),
            pltpu.VMEM((C * ROWS, MODES), jnp.float32),
            pltpu.VMEM((C * SUB, C * SUB), jnp.float32),
            pltpu.VMEM((WIDTH, MODES), bf16),
            pltpu.VMEM((MODES, WIDTH), bf16),
            pltpu.SemaphoreType.DMA((CHUNKS,)),
            pltpu.SemaphoreType.DMA((CHUNKS,)),
            pltpu.SemaphoreType.DMA((CHUNKS,)),
        ],
        compiler_params=limit(53),
        name="slope_and_modes",
    )(
        slab,
        field,
        cotangent,
        outer,
        inner,
        high,
        low,
        point_weight,
        bias.reshape(C, 1),
        *mixed_parts,
    )

    back, send = pl.pallas_call(
        back_kernel,
        out_shape=(shaped(OWNED, MODES), shaped(dp, 3 * SUB, LANES)),
        compiler_params=limit(8),
        name="back_modes",
    )(*reduce_parts(grad_parts), spec_weight, coef)

    got = lax.all_to_all(send, "dp", 0, 0, tiled=True)
    copies, point_grad, bias_grad = pl.pallas_call(
        functools.partial(
            outer_kernel, 1.0 / math.sqrt(dp * N), 1.0 / math.sqrt(dp * N * N * N)
        ),
        out_shape=(shaped(dp, SUB, SUB, LANES), shaped(C, C), shaped(1, C)),
        compiler_params=limit(8),
        name="sample_sum",
    )(got)
    owned = lax.all_to_all(copies, "dp", 0, 0, tiled=True)
    bias_grad, back = lax.optimization_barrier((bias_grad, back))
    two = flip(back, 2)
    back_parts = (back, flip(back, 1), two, flip(two, 1))

    field_grad = pl.pallas_call(
        functools.partial(field_grad_kernel, 768),
        out_shape=jax.ShapeDtypeStruct(field.shape, bf16),
        in_specs=[SM, ANY] + [VM] * 9,
        out_specs=ANY,
        scratch_shapes=[
            pltpu.VMEM((C * SUB, C * SUB), bf16),
            pltpu.VMEM((M * C, MODES), jnp.float32),
            pltpu.VMEM((C, ROWS, CELLS), bf16),
            pltpu.VMEM((C, ROWS, CELLS), bf16),
            pltpu.VMEM((C, ROWS, MODES), bf16),
            pltpu.VMEM((MODES, WIDTH), bf16),
            pltpu.SemaphoreType.DMA((CHUNKS,)),
            pltpu.SemaphoreType.DMA((CHUNKS,)),
        ],
        compiler_params=limit(54),
        cost_estimate=pl.CostEstimate(
            flops=2 * C * ROWS * CELLS * (MODES + C * SUB),
            bytes_accessed=2 * C * ROWS * CELLS * 2,
            transcendentals=0,
        ),
        name="field_grad",
    )(slab, dpre, outer, inner, high, low, point_weight, *back_parts)

    spec_grad = pl.pallas_call(
        place_kernel,
        out_shape=shaped(M // GZ, C, C, MODES),
        compiler_params=limit(8),
        name="place_pieces",
    )(owned)
    return field_grad, spec_grad, point_grad, bias_grad.reshape(C)


def solution(mesh):
    return jax.shard_map(
        shards,
        mesh=mesh,
        in_specs=(
            P("dp", None, "gz", None),
            P("dp", None, "gz", None),
            P("gz", None, None, None),
            P(),
            P(),
        ),
        out_specs=(P("dp", None, "gz", None), P("gz", None, None, None), P(), P()),
        check_vma=False,
    )
```

```python
import functools
import math

import jax
import jax.numpy as jnp
from jax import lax
from jax.experimental import pallas as pl
from jax.experimental.pallas import tpu as pltpu
from jax.sharding import PartitionSpec as P

N = 96
M = 16
C = 16
GZ = 4
ROWS = N // GZ
CELLS = N * N
MODES = M * M
OWNED = M // GZ * C
SUB = 8
LANES = 128
CHUNKS = 6
WIDTH = CELLS // CHUNKS

bf16 = jnp.bfloat16
root_half = 0.7071067811865476
density_norm = 0.3989422804014327
scale_fwd = (2.0 / N) ** 1.5
scale_inv = (2.0 / M) ** 1.5
HIGHEST = lax.Precision.HIGHEST
NN = (((1,), (0,)), ((), ()))
NT = (((1,), (1,)), ((), ()))
TN = (((0,), (0,)), ((), ()))


def gelu_slope(values):
    cumulative = 0.5 * (1.0 + lax.erf(values * root_half))
    return cumulative + values * jnp.exp(-0.5 * values * values) * density_norm


def matmul(a, b, dims=NN):
    return lax.dot_general(a, b, dims, preferred_element_type=jnp.float32)


def split(values):
    high = values.astype(bf16)
    return high, (values - high.astype(jnp.float32)).astype(bf16)


def product(a, b, dims):
    return matmul(a[0], b[0], dims) + (matmul(a[0], b[1], dims) + matmul(a[1], b[0], dims))


def iota(shape, dim):
    return lax.broadcasted_iota(jnp.int32, shape, dim)


def quotient(values, divisor):
    return jnp.floor((values + 0.5) * (1.0 / divisor))


def basis_at(mode, position):
    cosine = mode < M // 2
    frequency = jnp.where(cosine, mode, mode - (M // 2 - 1))
    turns = frequency * position + jnp.where(cosine, 0.0, 0.75 * N)
    turns = turns - N * quotient(turns, N)
    return jnp.cos(turns * (2.0 * math.pi / N))


def cell_tables():
    mode = iota((N, MODES), 1)
    cell = iota((N, MODES), 0).astype(jnp.float32)
    outer = basis_at((mode >> 4).astype(jnp.float32), cell)
    return outer, basis_at((mode & 15).astype(jnp.float32), cell)


def row_matrix(slab):
    col = iota((M, C * ROWS), 1).astype(jnp.float32)
    x = col - ROWS * quotient(col, ROWS) + (slab * ROWS).astype(jnp.float32)
    table = basis_at(iota((M, C * ROWS), 0).astype(jnp.float32), x)
    wide = jnp.broadcast_to(table[:, None, :], (M, C, C * ROWS)).reshape(M * C, C * ROWS)
    row_channel = (iota((M * C, C * ROWS), 0) & 15).astype(jnp.float32)
    col_channel = quotient(iota((M * C, C * ROWS), 1).astype(jnp.float32), ROWS)
    return jnp.where(row_channel == col_channel, wide, 0.0)


def one_hot_rows(dtype):
    hit = (iota((C * SUB, C), 0) >> 3) == iota((C * SUB, C), 1)
    return jnp.where(hit, 1.0, 0.0).astype(dtype)


def same_sub():
    return (iota((C * SUB, C * SUB), 0) & 7) == (iota((C * SUB, C * SUB), 1) & 7)


def spread(weight):
    hot = one_hot_rows(bf16)
    tall = matmul(hot, weight).astype(bf16)
    return jnp.where(same_sub(), matmul(tall, hot, NT), 0.0).astype(bf16)


def send_parts(slab, high_ref, low_ref, acc, scale, joined, refs):
    joined[...] = scale * product((high_ref[...], low_ref[...]), split(acc), NN)
    for k in range(GZ):
        first = pl.multiple_of((slab ^ k) * OWNED, OWNED)
        refs[k][0:OWNED, :] = joined[pl.ds(first, OWNED), :]


def chunk(step):
    if isinstance(step, int):
        return slice(step * WIDTH, (step + 1) * WIDTH)
    return pl.ds(pl.multiple_of(step * WIDTH, LANES), WIDTH)


def copies_in(source, target, sems):
    def copy(step):
        cols = chunk(step)
        return pltpu.make_async_copy(
            source.at[0, :, :, cols], target.at[:, :, cols], sems.at[step]
        )

    return copy


def copies_out(source, target, sems):
    def copy(step):
        cols = chunk(step)
        return pltpu.make_async_copy(
            source.at[:, :, cols], target.at[0, :, :, cols], sems.at[step]
        )

    return copy


def kron_rows(outer, inner, step):
    table = inner[...]
    rows = [
        (outer[pl.ds(step * (WIDTH // N) + k, 1), :] * table).astype(bf16)
        for k in range(WIDTH // N)
    ]
    return jnp.concatenate(rows, 0)


def field_modes_kernel(slab_ref, field_hbm, *rest):
    parts = rest[:GZ]
    outer, inner, high, low, field, acc, joined, sems = rest[GZ:]
    fetch = copies_in(field_hbm, field, sems)
    for step in range(CHUNKS):
        fetch(step).start()
    outer[...], inner[...] = cell_tables()
    high[...], low[...] = split(row_matrix(slab_ref[0]))
    acc[...] = jnp.zeros_like(acc)

    def body(step, carry):
        kron = kron_rows(outer, inner, step)
        fetch(step).wait()
        acc[...] += matmul(field[:, :, chunk(step)].reshape(C * ROWS, WIDTH), kron)
        return carry

    lax.fori_loop(0, CHUNKS, body, 0)
    send_parts(slab_ref[0], high, low, acc[...], scale_fwd, joined, parts)


def join_parts(slab, refs, joined):
    for k, ref in enumerate(refs):
        joined[pl.ds(pl.multiple_of((slab ^ k) * OWNED, OWNED), OWNED), :] = ref[...]


def slope_kernel(
    sub_width,
    slab_ref,
    field_hbm,
    cot_hbm,
    weight_ref,
    bias_ref,
    own_ref,
    one_ref,
    two_ref,
    three_ref,
    dpre_hbm,
    *rest,
):
    parts = rest[:GZ]
    outer, inner, high, low, mixed, down, bias_cols, field, cot, out, lines, acc, point_acc, kron, kron_t, *sems = rest[GZ:]
    field_sems, cot_sems, out_sems = sems
    fetch_field = copies_in(field_hbm, field, field_sems)
    fetch_cot = copies_in(cot_hbm, cot, cot_sems)
    store = copies_out(out, dpre_hbm, out_sems)
    for step in range(CHUNKS):
        fetch_field(step).start()
        fetch_cot(step).start()
    outer[...], inner[...] = cell_tables()
    high[...], low[...] = split(row_matrix(slab_ref[0]))
    down[...] = spread(weight_ref[...].T)
    bias_high, bias_low = split(
        jnp.dot(
            one_hot_rows(jnp.float32),
            bias_ref[...],
            precision=HIGHEST,
            preferred_element_type=jnp.float32,
        )
    )
    lane = iota((C * SUB, C), 1)
    bias_cols[...] = jnp.where(
        lane == 0,
        bias_high.astype(jnp.float32),
        jnp.where(lane == 1, bias_low.astype(jnp.float32), 0.0),
    ).astype(bf16)
    ones = jnp.ones((C, sub_width), bf16)
    join_parts(slab_ref[0], (own_ref, one_ref, two_ref, three_ref), mixed)
    full = product((high[...], low[...]), split(mixed[...]), TN)
    lines[...] = (scale_inv * full).reshape(C, ROWS, MODES).astype(bf16)
    acc[...] = jnp.zeros_like(acc)
    point_acc[...] = jnp.zeros_like(point_acc)

    for step in range(CHUNKS):
        kron[...] = kron_rows(outer, inner, step)
        kron_t[...] = kron[...].T
        fetch_field(step).wait()
        fetch_cot(step).wait()
        for s in range(WIDTH // sub_width):
            cols = slice(step * WIDTH + s * sub_width, step * WIDTH + (s + 1) * sub_width)
            table = kron_t[:, s * sub_width : (s + 1) * sub_width]
            for x in range(ROWS // SUB):
                rows = slice(x * SUB, (x + 1) * SUB)
                values = field[:, rows, cols].reshape(C * SUB, sub_width)
                left = jnp.concatenate(
                    [lines[:, rows, :].reshape(C * SUB, MODES), down[...], bias_cols[...]], 1
                )
                pre = matmul(left, jnp.concatenate([table, values, ones], 0))
                grad = cot[:, rows, cols].reshape(C * SUB, sub_width).astype(jnp.float32)
                dpre = (grad * gelu_slope(pre)).astype(bf16)
                out[:, rows, cols] = dpre.reshape(C, SUB, sub_width)
        store(step).start()
        cols = chunk(step)
        for x in range(ROWS // SUB):
            rows = slice(x * SUB, (x + 1) * SUB)
            point_acc[...] += matmul(
                field[:, rows, cols].reshape(C * SUB, WIDTH),
                out[:, rows, cols].reshape(C * SUB, WIDTH),
                NT,
            )
        acc[...] += matmul(out[:, :, cols].reshape(C * ROWS, WIDTH), kron[...])
    send_parts(slab_ref[0], high, low, acc[...], scale_inv, mixed, parts)
    sums = acc[:, 0:LANES].reshape(C, ROWS, LANES).sum(1)[:, 0:1]
    packed = pack_small(point_acc[...], sums)
    for k in range(GZ):
        parts[k][OWNED : OWNED + SUB, 0:LANES] = packed
        parts[k][OWNED : OWNED + SUB, LANES:MODES] = jnp.zeros_like(packed)
    for step in range(CHUNKS):
        store(step).wait()


def lane_masks():
    return iota((C, LANES), 0), iota((C, LANES), 1)


def pack_small(blocks, sums):
    fold = jnp.where((iota((C * SUB, LANES), 0) >> 3) == (iota((C * SUB, LANES), 1) & 15), 1.0, 0.0)
    fold = fold.astype(bf16)
    high, low = split(jnp.where(same_sub(), blocks, 0.0))
    wide = matmul(high, fold) + matmul(low, fold)
    channel = (iota((C * SUB, LANES), 0) >> 3) & 7
    wide = jnp.where(channel == (iota((C * SUB, LANES), 1) >> 4), wide, 0.0)
    first = wide[0 : 8 * SUB].sum(0, keepdims=True)
    second = wide[8 * SUB :].sum(0, keepdims=True)
    row, lane = lane_masks()
    vector = jnp.where(row == lane, sums, 0.0).sum(0, keepdims=True)
    return jnp.concatenate([first, second, vector, jnp.zeros((5, LANES), jnp.float32)], 0)


def unpack_small(packed):
    row, lane = lane_masks()
    wide = jnp.where(row < 8, packed[0:1], packed[1:2])
    wide = jnp.where((row & 7) == (lane >> 4), wide, 0.0)
    tile = jnp.where((lane & 15) == row, 1.0, 0.0)
    point = lax.dot_general(wide, tile, NT, precision=HIGHEST, preferred_element_type=jnp.float32)
    return point, packed[2:3, 0:C]


def add_kernel(a_ref, b_ref, out_ref):
    out_ref[...] = a_ref[...] + b_ref[...]


def mix_kernel(own_ref, one_ref, two_ref, weight_ref, coef_ref, mixed_ref):
    coef_ref[...] = (own_ref[...] + one_ref[...]) + two_ref[...]
    for a in range(M // GZ):
        total = jnp.zeros((C, MODES), jnp.float32)
        for i in range(C):
            total = total + coef_ref[a * C + i : a * C + i + 1, :] * weight_ref[a, i]
        mixed_ref[a * C : (a + 1) * C, :] = total


def pieces():
    for owner in range(M // GZ * 8):
        yield owner, owner // 8, owner // 4 % 2 * SUB, owner // 2 % 2 * SUB, owner % 2 * LANES


def back_kernel(own_ref, one_ref, two_ref, weight_ref, coef_ref, back_ref, send_ref):
    full = (own_ref[...] + one_ref[...]) + two_ref[...]
    small = full[OWNED : OWNED + SUB, 0:LANES]
    for owner, a, i, o, p in pieces():
        send_ref[owner, 0:SUB, :] = coef_ref[a * C + i : a * C + i + SUB, p : p + LANES]
        send_ref[owner, SUB : 2 * SUB, :] = full[a * C + o : a * C + o + SUB, p : p + LANES]
        send_ref[owner, 2 * SUB : 3 * SUB, :] = small
    for a in range(M // GZ):
        grad = full[a * C : (a + 1) * C]
        for i in range(C):
            back_ref[a * C + i : a * C + i + 1, :] = (weight_ref[a, i] * grad).sum(
                0, keepdims=True
            )


def outer_kernel(spec_norm, cell_norm, got_ref, copies_ref, point_ref, bias_ref):
    samples = got_ref.shape[0]

    def body(s, carry):
        *totals, small = carry
        coef = got_ref[s, 0:SUB, :]
        grad = got_ref[s, SUB : 2 * SUB, :]
        totals = [total + coef[i : i + 1] * grad for i, total in enumerate(totals)]
        return (*totals, small + got_ref[s, 2 * SUB : 3 * SUB, :])

    zero = jnp.zeros((SUB, LANES), jnp.float32)
    *totals, small = lax.fori_loop(0, samples, body, (zero,) * (SUB + 1), unroll=8)
    for i, total in enumerate(totals):
        scaled = total * spec_norm
        for k in range(samples):
            copies_ref[k, i] = scaled
    point, sums = unpack_small(small)
    point_ref[...] = point * cell_norm
    bias_ref[...] = sums * cell_norm


def place_kernel(got_ref, out_ref):
    for owner, a, i, o, p in pieces():
        out_ref[a, i : i + SUB, o : o + SUB, p : p + LANES] = got_ref[owner]


def field_grad_kernel(
    sub_width,
    slab_ref,
    dpre_hbm,
    weight_ref,
    own_ref,
    one_ref,
    two_ref,
    three_ref,
    out_hbm,
    outer,
    inner,
    up,
    back,
    dpre,
    out,
    lines,
    kron_t,
    dpre_sems,
    out_sems,
):
    fetch = copies_in(dpre_hbm, dpre, dpre_sems)
    store = copies_out(out, out_hbm, out_sems)
    for step in range(CHUNKS):
        fetch(step).start()
    outer[...], inner[...] = cell_tables()
    up[...] = spread(weight_ref[...])
    join_parts(slab_ref[0], (own_ref, one_ref, two_ref, three_ref), back)
    full = product(split(row_matrix(slab_ref[0])), split(back[...]), TN)
    lines[...] = (scale_fwd * full).reshape(C, ROWS, MODES).astype(bf16)

    for step in range(CHUNKS):
        kron_t[...] = kron_rows(outer, inner, step).T
        fetch(step).wait()
        for s in range(WIDTH // sub_width):
            cols = slice(step * WIDTH + s * sub_width, step * WIDTH + (s + 1) * sub_width)
            table = kron_t[:, s * sub_width : (s + 1) * sub_width]
            for x in range(ROWS // SUB):
                rows = slice(x * SUB, (x + 1) * SUB)
                values = dpre[:, rows, cols].reshape(C * SUB, sub_width)
                left = jnp.concatenate([lines[:, rows, :].reshape(C * SUB, MODES), up[...]], 1)
                grad = matmul(left, jnp.concatenate([table, values], 0))
                out[:, rows, cols] = grad.astype(bf16).reshape(C, SUB, sub_width)
        store(step).start()
    for step in range(CHUNKS):
        store(step).wait()


def shaped(*shape, dtype=jnp.float32):
    return jax.ShapeDtypeStruct(shape, dtype)


def limit(mebibytes):
    return pltpu.CompilerParams(vmem_limit_bytes=mebibytes << 20)


VM = pl.BlockSpec(memory_space=pltpu.VMEM)
SM = pl.BlockSpec(memory_space=pltpu.SMEM)
ANY = pl.BlockSpec(memory_space=pl.ANY)


def shards(field, cotangent, spec_weight, point_weight, bias):
    dp = lax.axis_size("dp")
    slab = lax.axis_index("gz").astype(jnp.int32).reshape(1)

    def flip(values, k):
        return lax.ppermute(values, "gz", [(g, g ^ k) for g in range(GZ)])

    def reduce_parts(parts):
        three = flip(parts[3], 1)
        one = flip(parts[1], 1)
        forward = pl.pallas_call(
            add_kernel,
            out_shape=jax.ShapeDtypeStruct(three.shape, three.dtype),
            compiler_params=limit(8),
            name="add_pair",
        )(parts[2], three)
        return parts[0], one, flip(forward, 2)

    coef_parts = pl.pallas_call(
        field_modes_kernel,
        out_shape=tuple(shaped(OWNED, MODES) for _ in range(GZ)),
        in_specs=[SM, ANY],
        out_specs=(VM,) * GZ,
        scratch_shapes=[
            pltpu.VMEM((N, MODES), jnp.float32),
            pltpu.VMEM((N, MODES), jnp.float32),
            pltpu.VMEM((M * C, C * ROWS), bf16),
            pltpu.VMEM((M * C, C * ROWS), bf16),
            pltpu.VMEM((C, ROWS, CELLS), bf16),
            pltpu.VMEM((C * ROWS, MODES), jnp.float32),
            pltpu.VMEM((M * C, MODES), jnp.float32),
            pltpu.SemaphoreType.DMA((CHUNKS,)),
        ],
        compiler_params=limit(53),
        name="field_modes",
    )(slab, field)

    coef, mixed = pl.pallas_call(
        mix_kernel,
        out_shape=(shaped(OWNED, MODES), shaped(OWNED, MODES)),
        compiler_params=limit(8),
        name="mix_modes",
    )(*reduce_parts(coef_parts), spec_weight)
    mixed_two = flip(mixed, 2)
    mixed_parts = (mixed, flip(mixed, 1), mixed_two, flip(mixed_two, 1))

    dpre, *grad_parts = pl.pallas_call(
        functools.partial(slope_kernel, 768),
        out_shape=(jax.ShapeDtypeStruct(field.shape, bf16),)
        + tuple(shaped(OWNED + SUB, MODES) for _ in range(GZ)),
        in_specs=[SM, ANY, ANY] + [VM] * 6,
        out_specs=(ANY,) + (VM,) * GZ,
        scratch_shapes=[
            pltpu.VMEM((N, MODES), jnp.float32),
            pltpu.VMEM((N, MODES), jnp.float32),
            pltpu.VMEM((M * C, C * ROWS), bf16),
            pltpu.VMEM((M * C, C * ROWS), bf16),
            pltpu.VMEM((M * C, MODES), jnp.float32),
            pltpu.VMEM((C * SUB, C * SUB), bf16),
            pltpu.VMEM((C * SUB, C), bf16),
            pltpu.VMEM((C, ROWS, CELLS), bf16),
            pltpu.VMEM((C, ROWS, CELLS), bf16),
            pltpu.VMEM((C, ROWS, CELLS), bf16),
            pltpu.VMEM((C, ROWS, MODES), bf16),
            pltpu.VMEM((C * ROWS, MODES), jnp.float32),
            pltpu.VMEM((C * SUB, C * SUB), jnp.float32),
            pltpu.VMEM((WIDTH, MODES), bf16),
            pltpu.VMEM((MODES, WIDTH), bf16),
            pltpu.SemaphoreType.DMA((CHUNKS,)),
            pltpu.SemaphoreType.DMA((CHUNKS,)),
            pltpu.SemaphoreType.DMA((CHUNKS,)),
        ],
        compiler_params=limit(53),
        name="slope_and_modes",
    )(
        slab,
        field,
        cotangent,
        point_weight,
        bias.reshape(C, 1),
        *mixed_parts,
    )

    back, send = pl.pallas_call(
        back_kernel,
        out_shape=(shaped(OWNED, MODES), shaped(dp, 3 * SUB, LANES)),
        compiler_params=limit(8),
        name="back_modes",
    )(*reduce_parts(grad_parts), spec_weight, coef)

    got = lax.all_to_all(send, "dp", 0, 0, tiled=True)
    two = flip(back, 2)
    back_parts = (back, flip(back, 1), two, flip(two, 1))
    copies, point_grad, bias_grad = pl.pallas_call(
        functools.partial(
            outer_kernel, 1.0 / math.sqrt(dp * N), 1.0 / math.sqrt(dp * N * N * N)
        ),
        out_shape=(shaped(dp, SUB, SUB, LANES), shaped(C, C), shaped(1, C)),
        compiler_params=limit(8),
        name="sample_sum",
    )(got)
    copies, *back_parts = lax.optimization_barrier((copies, *back_parts))
    owned = lax.all_to_all(copies, "dp", 0, 0, tiled=True)

    field_grad = pl.pallas_call(
        functools.partial(field_grad_kernel, 768),
        out_shape=jax.ShapeDtypeStruct(field.shape, bf16),
        in_specs=[SM, ANY] + [VM] * 5,
        out_specs=ANY,
        scratch_shapes=[
            pltpu.VMEM((N, MODES), jnp.float32),
            pltpu.VMEM((N, MODES), jnp.float32),
            pltpu.VMEM((C * SUB, C * SUB), bf16),
            pltpu.VMEM((M * C, MODES), jnp.float32),
            pltpu.VMEM((C, ROWS, CELLS), bf16),
            pltpu.VMEM((C, ROWS, CELLS), bf16),
            pltpu.VMEM((C, ROWS, MODES), bf16),
            pltpu.VMEM((MODES, WIDTH), bf16),
            pltpu.SemaphoreType.DMA((CHUNKS,)),
            pltpu.SemaphoreType.DMA((CHUNKS,)),
        ],
        compiler_params=limit(54),
        cost_estimate=pl.CostEstimate(
            flops=2 * C * ROWS * CELLS * (MODES + C * SUB),
            bytes_accessed=2 * C * ROWS * CELLS * 2,
            transcendentals=0,
        ),
        name="field_grad",
    )(slab, dpre, point_weight, *back_parts)

    spec_grad = pl.pallas_call(
        place_kernel,
        out_shape=shaped(M // GZ, C, C, MODES),
        compiler_params=limit(8),
        name="place_pieces",
    )(owned)
    return field_grad, spec_grad, point_grad, bias_grad.reshape(C)


def solution(mesh):
    return jax.shard_map(
        shards,
        mesh=mesh,
        in_specs=(
            P("dp", None, "gz", None),
            P("dp", None, "gz", None),
            P("gz", None, None, None),
            P(),
            P(),
        ),
        out_specs=(P("dp", None, "gz", None), P("gz", None, None, None), P(), P()),
        check_vma=False,
    )
```

```python
import functools
import math

import jax
import jax.numpy as jnp
from jax import lax
from jax.experimental import pallas as pl
from jax.experimental.pallas import tpu as pltpu
from jax.sharding import PartitionSpec as P

N = 96
M = 16
C = 16
GZ = 4
ROWS = N // GZ
CELLS = N * N
MODES = M * M
OWNED = M // GZ * C
SUB = 8
LANES = 128
CHUNKS = 6
WIDTH = CELLS // CHUNKS

bf16 = jnp.bfloat16
root_half = 0.7071067811865476
density_norm = 0.3989422804014327
scale_fwd = (2.0 / N) ** 1.5
scale_inv = (2.0 / M) ** 1.5
HIGHEST = lax.Precision.HIGHEST
NN = (((1,), (0,)), ((), ()))
NT = (((1,), (1,)), ((), ()))
TN = (((0,), (0,)), ((), ()))


def gelu_slope(values):
    cumulative = 0.5 * (1.0 + lax.erf(values * root_half))
    return cumulative + values * jnp.exp(-0.5 * values * values) * density_norm


def matmul(a, b, dims=NN):
    return lax.dot_general(a, b, dims, preferred_element_type=jnp.float32)


def split(values):
    high = values.astype(bf16)
    return high, (values - high.astype(jnp.float32)).astype(bf16)


def product(a, b, dims):
    return matmul(a[0], b[0], dims) + (matmul(a[0], b[1], dims) + matmul(a[1], b[0], dims))


def iota(shape, dim):
    return lax.broadcasted_iota(jnp.int32, shape, dim)


def quotient(values, divisor):
    return jnp.floor((values + 0.5) * (1.0 / divisor))


def basis_at(mode, position):
    cosine = mode < M // 2
    frequency = jnp.where(cosine, mode, mode - (M // 2 - 1))
    turns = frequency * position + jnp.where(cosine, 0.0, 0.75 * N)
    turns = turns - N * quotient(turns, N)
    return jnp.cos(turns * (2.0 * math.pi / N))


def cell_tables():
    mode = iota((N, MODES), 1)
    cell = iota((N, MODES), 0).astype(jnp.float32)
    outer = basis_at((mode >> 4).astype(jnp.float32), cell)
    return outer, basis_at((mode & 15).astype(jnp.float32), cell)


def row_matrix(slab):
    col = iota((M, C * ROWS), 1).astype(jnp.float32)
    x = col - ROWS * quotient(col, ROWS) + (slab * ROWS).astype(jnp.float32)
    table = basis_at(iota((M, C * ROWS), 0).astype(jnp.float32), x)
    wide = jnp.broadcast_to(table[:, None, :], (M, C, C * ROWS)).reshape(M * C, C * ROWS)
    row_channel = (iota((M * C, C * ROWS), 0) & 15).astype(jnp.float32)
    col_channel = quotient(iota((M * C, C * ROWS), 1).astype(jnp.float32), ROWS)
    return jnp.where(row_channel == col_channel, wide, 0.0)


def one_hot_rows(dtype):
    hit = (iota((C * SUB, C), 0) >> 3) == iota((C * SUB, C), 1)
    return jnp.where(hit, 1.0, 0.0).astype(dtype)


def same_sub():
    return (iota((C * SUB, C * SUB), 0) & 7) == (iota((C * SUB, C * SUB), 1) & 7)


def spread(weight):
    hot = one_hot_rows(bf16)
    tall = matmul(hot, weight).astype(bf16)
    return jnp.where(same_sub(), matmul(tall, hot, NT), 0.0).astype(bf16)


def send_parts(slab, high_ref, low_ref, acc, scale, joined, refs):
    joined[...] = scale * product((high_ref[...], low_ref[...]), split(acc), NN)
    for k in range(GZ):
        first = pl.multiple_of((slab ^ k) * OWNED, OWNED)
        refs[k][0:OWNED, :] = joined[pl.ds(first, OWNED), :]


def chunk(step):
    if isinstance(step, int):
        return slice(step * WIDTH, (step + 1) * WIDTH)
    return pl.ds(pl.multiple_of(step * WIDTH, LANES), WIDTH)


def copies_in(source, target, sems):
    def copy(step):
        cols = chunk(step)
        return pltpu.make_async_copy(
            source.at[0, :, :, cols], target.at[:, :, cols], sems.at[step]
        )

    return copy


def copies_out(source, target, sems):
    def copy(step):
        cols = chunk(step)
        return pltpu.make_async_copy(
            source.at[:, :, cols], target.at[0, :, :, cols], sems.at[step]
        )

    return copy


def kron_rows(outer, inner, step):
    table = inner[...]
    rows = [
        (outer[pl.ds(step * (WIDTH // N) + k, 1), :] * table).astype(bf16)
        for k in range(WIDTH // N)
    ]
    return jnp.concatenate(rows, 0)


def field_modes_kernel(slab_ref, field_hbm, *rest):
    parts = rest[:GZ]
    outer, inner, high, low, field, acc, joined, sems = rest[GZ:]
    fetch = copies_in(field_hbm, field, sems)
    for step in range(CHUNKS):
        fetch(step).start()
    outer[...], inner[...] = cell_tables()
    high[...], low[...] = split(row_matrix(slab_ref[0]))
    acc[...] = jnp.zeros_like(acc)

    def body(step, carry):
        kron = kron_rows(outer, inner, step)
        fetch(step).wait()
        acc[...] += matmul(field[:, :, chunk(step)].reshape(C * ROWS, WIDTH), kron)
        return carry

    lax.fori_loop(0, CHUNKS, body, 0)
    send_parts(slab_ref[0], high, low, acc[...], scale_fwd, joined, parts)


def join_parts(slab, refs, joined):
    for k, ref in enumerate(refs):
        joined[pl.ds(pl.multiple_of((slab ^ k) * OWNED, OWNED), OWNED), :] = ref[...]


def slope_kernel(
    sub_width,
    slab_ref,
    field_hbm,
    cot_hbm,
    weight_ref,
    bias_ref,
    own_ref,
    one_ref,
    two_ref,
    three_ref,
    dpre_hbm,
    *rest,
):
    parts = rest[:GZ]
    outer, inner, high, low, mixed, down, bias_cols, field, cot, out, lines, acc, point_acc, kron, kron_t, *sems = rest[GZ:]
    field_sems, cot_sems, out_sems = sems
    fetch_field = copies_in(field_hbm, field, field_sems)
    fetch_cot = copies_in(cot_hbm, cot, cot_sems)
    store = copies_out(out, dpre_hbm, out_sems)
    for step in range(CHUNKS):
        fetch_field(step).start()
        fetch_cot(step).start()
    outer[...], inner[...] = cell_tables()
    high[...], low[...] = split(row_matrix(slab_ref[0]))
    down[...] = spread(weight_ref[...].T)
    bias_high, bias_low = split(
        jnp.dot(
            one_hot_rows(jnp.float32),
            bias_ref[...],
            precision=HIGHEST,
            preferred_element_type=jnp.float32,
        )
    )
    lane = iota((C * SUB, C), 1)
    bias_cols[...] = jnp.where(
        lane == 0,
        bias_high.astype(jnp.float32),
        jnp.where(lane == 1, bias_low.astype(jnp.float32), 0.0),
    ).astype(bf16)
    ones = jnp.ones((C, sub_width), bf16)
    join_parts(slab_ref[0], (own_ref, one_ref, two_ref, three_ref), mixed)
    full = product((high[...], low[...]), split(mixed[...]), TN)
    lines[...] = (scale_inv * full).reshape(C, ROWS, MODES).astype(bf16)
    acc[...] = jnp.zeros_like(acc)
    point_acc[...] = jnp.zeros_like(point_acc)

    for step in range(CHUNKS):
        kron[...] = kron_rows(outer, inner, step)
        kron_t[...] = kron[...].T
        fetch_field(step).wait()
        fetch_cot(step).wait()
        for s in range(WIDTH // sub_width):
            cols = slice(step * WIDTH + s * sub_width, step * WIDTH + (s + 1) * sub_width)
            table = kron_t[:, s * sub_width : (s + 1) * sub_width]
            for x in range(ROWS // SUB):
                rows = slice(x * SUB, (x + 1) * SUB)
                values = field[:, rows, cols].reshape(C * SUB, sub_width)
                left = jnp.concatenate(
                    [lines[:, rows, :].reshape(C * SUB, MODES), down[...], bias_cols[...]], 1
                )
                pre = matmul(left, jnp.concatenate([table, values, ones], 0))
                grad = cot[:, rows, cols].reshape(C * SUB, sub_width).astype(jnp.float32)
                dpre = (grad * gelu_slope(pre)).astype(bf16)
                out[:, rows, cols] = dpre.reshape(C, SUB, sub_width)
        store(step).start()
        cols = chunk(step)
        for x in range(ROWS // SUB):
            rows = slice(x * SUB, (x + 1) * SUB)
            point_acc[...] += matmul(
                field[:, rows, cols].reshape(C * SUB, WIDTH),
                out[:, rows, cols].reshape(C * SUB, WIDTH),
                NT,
            )
        acc[...] += matmul(out[:, :, cols].reshape(C * ROWS, WIDTH), kron[...])
    send_parts(slab_ref[0], high, low, acc[...], scale_inv, mixed, parts)
    sums = acc[:, 0:LANES].reshape(C, ROWS, LANES).sum(1)[:, 0:1]
    packed = pack_small(point_acc[...], sums)
    for k in range(GZ):
        parts[k][OWNED : OWNED + SUB, 0:LANES] = packed
        parts[k][OWNED : OWNED + SUB, LANES:MODES] = jnp.zeros_like(packed)
    for step in range(CHUNKS):
        store(step).wait()


def lane_masks():
    return iota((C, LANES), 0), iota((C, LANES), 1)


def pack_small(blocks, sums):
    fold = jnp.where((iota((C * SUB, LANES), 0) >> 3) == (iota((C * SUB, LANES), 1) & 15), 1.0, 0.0)
    fold = fold.astype(bf16)
    high, low = split(jnp.where(same_sub(), blocks, 0.0))
    wide = matmul(high, fold) + matmul(low, fold)
    channel = (iota((C * SUB, LANES), 0) >> 3) & 7
    wide = jnp.where(channel == (iota((C * SUB, LANES), 1) >> 4), wide, 0.0)
    first = wide[0 : 8 * SUB].sum(0, keepdims=True)
    second = wide[8 * SUB :].sum(0, keepdims=True)
    row, lane = lane_masks()
    vector = jnp.where(row == lane, sums, 0.0).sum(0, keepdims=True)
    return jnp.concatenate([first, second, vector, jnp.zeros((5, LANES), jnp.float32)], 0)


def unpack_small(packed):
    row, lane = lane_masks()
    wide = jnp.where(row < 8, packed[0:1], packed[1:2])
    wide = jnp.where((row & 7) == (lane >> 4), wide, 0.0)
    tile = jnp.where((lane & 15) == row, 1.0, 0.0)
    point = lax.dot_general(wide, tile, NT, precision=HIGHEST, preferred_element_type=jnp.float32)
    return point, packed[2:3, 0:C]


def add_kernel(a_ref, b_ref, out_ref):
    out_ref[...] = a_ref[...] + b_ref[...]


def mix_kernel(own_ref, one_ref, two_ref, weight_ref, coef_ref, mixed_ref):
    coef_ref[...] = (own_ref[...] + one_ref[...]) + two_ref[...]
    for a in range(M // GZ):
        total = jnp.zeros((C, MODES), jnp.float32)
        for i in range(C):
            total = total + coef_ref[a * C + i : a * C + i + 1, :] * weight_ref[a, i]
        mixed_ref[a * C : (a + 1) * C, :] = total


def pieces():
    for owner in range(M // GZ * 8):
        yield owner, owner // 8, owner // 4 % 2 * SUB, owner // 2 % 2 * SUB, owner % 2 * LANES


def send_kernel(own_ref, one_ref, two_ref, coef_ref, full_ref, send_ref):
    full = (own_ref[...] + one_ref[...]) + two_ref[...]
    full_ref[...] = full
    small = full[OWNED : OWNED + SUB, 0:LANES]
    for owner, a, i, o, p in pieces():
        send_ref[owner, 0:SUB, :] = coef_ref[a * C + i : a * C + i + SUB, p : p + LANES]
        send_ref[owner, SUB : 2 * SUB, :] = full[a * C + o : a * C + o + SUB, p : p + LANES]
        send_ref[owner, 2 * SUB : 3 * SUB, :] = small


def back_kernel(full_ref, weight_ref, back_ref):
    for a in range(M // GZ):
        grad = full_ref[a * C : (a + 1) * C]
        for i in range(C):
            back_ref[a * C + i : a * C + i + 1, :] = (weight_ref[a, i] * grad).sum(
                0, keepdims=True
            )


def outer_kernel(spec_norm, cell_norm, got_ref, copies_ref, point_ref, bias_ref):
    samples = got_ref.shape[0]

    def body(s, carry):
        *totals, small = carry
        coef = got_ref[s, 0:SUB, :]
        grad = got_ref[s, SUB : 2 * SUB, :]
        totals = [total + coef[i : i + 1] * grad for i, total in enumerate(totals)]
        return (*totals, small + got_ref[s, 2 * SUB : 3 * SUB, :])

    zero = jnp.zeros((SUB, LANES), jnp.float32)
    *totals, small = lax.fori_loop(0, samples, body, (zero,) * (SUB + 1), unroll=8)
    for i, total in enumerate(totals):
        scaled = total * spec_norm
        for k in range(samples):
            copies_ref[k, i] = scaled
    point, sums = unpack_small(small)
    point_ref[...] = point * cell_norm
    bias_ref[...] = sums * cell_norm


def place_kernel(got_ref, out_hbm, sems):
    copies = [
        pltpu.make_async_copy(
            got_ref.at[owner],
            out_hbm.at[a, i : i + SUB, o : o + SUB, p : p + LANES],
            sems.at[owner],
        )
        for owner, a, i, o, p in pieces()
    ]
    for copy in copies:
        copy.start()
    for copy in copies:
        copy.wait()


def field_grad_kernel(
    sub_width,
    slab_ref,
    dpre_hbm,
    weight_ref,
    own_ref,
    one_ref,
    two_ref,
    three_ref,
    out_hbm,
    outer,
    inner,
    up,
    back,
    dpre,
    out,
    lines,
    kron_t,
    dpre_sems,
    out_sems,
):
    fetch = copies_in(dpre_hbm, dpre, dpre_sems)
    store = copies_out(out, out_hbm, out_sems)
    for step in range(CHUNKS):
        fetch(step).start()
    outer[...], inner[...] = cell_tables()
    up[...] = spread(weight_ref[...])
    join_parts(slab_ref[0], (own_ref, one_ref, two_ref, three_ref), back)
    full = product(split(row_matrix(slab_ref[0])), split(back[...]), TN)
    lines[...] = (scale_fwd * full).reshape(C, ROWS, MODES).astype(bf16)

    for step in range(CHUNKS):
        kron_t[...] = kron_rows(outer, inner, step).T
        fetch(step).wait()
        for s in range(WIDTH // sub_width):
            cols = slice(step * WIDTH + s * sub_width, step * WIDTH + (s + 1) * sub_width)
            table = kron_t[:, s * sub_width : (s + 1) * sub_width]
            for x in range(ROWS // SUB):
                rows = slice(x * SUB, (x + 1) * SUB)
                values = dpre[:, rows, cols].reshape(C * SUB, sub_width)
                left = jnp.concatenate([lines[:, rows, :].reshape(C * SUB, MODES), up[...]], 1)
                grad = matmul(left, jnp.concatenate([table, values], 0))
                out[:, rows, cols] = grad.astype(bf16).reshape(C, SUB, sub_width)
        store(step).start()
    for step in range(CHUNKS):
        store(step).wait()


def shaped(*shape, dtype=jnp.float32):
    return jax.ShapeDtypeStruct(shape, dtype)


def limit(mebibytes):
    return pltpu.CompilerParams(vmem_limit_bytes=mebibytes << 20)


VM = pl.BlockSpec(memory_space=pltpu.VMEM)
SM = pl.BlockSpec(memory_space=pltpu.SMEM)
ANY = pl.BlockSpec(memory_space=pl.ANY)


def shards(field, cotangent, spec_weight, point_weight, bias):
    dp = lax.axis_size("dp")
    slab = lax.axis_index("gz").astype(jnp.int32).reshape(1)

    def flip(values, k):
        return lax.ppermute(values, "gz", [(g, g ^ k) for g in range(GZ)])

    def reduce_parts(parts):
        three = flip(parts[3], 1)
        one = flip(parts[1], 1)
        forward = pl.pallas_call(
            add_kernel,
            out_shape=jax.ShapeDtypeStruct(three.shape, three.dtype),
            compiler_params=limit(8),
            name="add_pair",
        )(parts[2], three)
        return parts[0], one, flip(forward, 2)

    coef_parts = pl.pallas_call(
        field_modes_kernel,
        out_shape=tuple(shaped(OWNED, MODES) for _ in range(GZ)),
        in_specs=[SM, ANY],
        out_specs=(VM,) * GZ,
        scratch_shapes=[
            pltpu.VMEM((N, MODES), jnp.float32),
            pltpu.VMEM((N, MODES), jnp.float32),
            pltpu.VMEM((M * C, C * ROWS), bf16),
            pltpu.VMEM((M * C, C * ROWS), bf16),
            pltpu.VMEM((C, ROWS, CELLS), bf16),
            pltpu.VMEM((C * ROWS, MODES), jnp.float32),
            pltpu.VMEM((M * C, MODES), jnp.float32),
            pltpu.SemaphoreType.DMA((CHUNKS,)),
        ],
        compiler_params=limit(53),
        name="field_modes",
    )(slab, field)

    coef, mixed = pl.pallas_call(
        mix_kernel,
        out_shape=(shaped(OWNED, MODES), shaped(OWNED, MODES)),
        compiler_params=limit(8),
        name="mix_modes",
    )(*reduce_parts(coef_parts), spec_weight)
    mixed_two = flip(mixed, 2)
    mixed_parts = (mixed, flip(mixed, 1), mixed_two, flip(mixed_two, 1))

    dpre, *grad_parts = pl.pallas_call(
        functools.partial(slope_kernel, 768),
        out_shape=(jax.ShapeDtypeStruct(field.shape, bf16),)
        + tuple(shaped(OWNED + SUB, MODES) for _ in range(GZ)),
        in_specs=[SM, ANY, ANY] + [VM] * 6,
        out_specs=(ANY,) + (VM,) * GZ,
        scratch_shapes=[
            pltpu.VMEM((N, MODES), jnp.float32),
            pltpu.VMEM((N, MODES), jnp.float32),
            pltpu.VMEM((M * C, C * ROWS), bf16),
            pltpu.VMEM((M * C, C * ROWS), bf16),
            pltpu.VMEM((M * C, MODES), jnp.float32),
            pltpu.VMEM((C * SUB, C * SUB), bf16),
            pltpu.VMEM((C * SUB, C), bf16),
            pltpu.VMEM((C, ROWS, CELLS), bf16),
            pltpu.VMEM((C, ROWS, CELLS), bf16),
            pltpu.VMEM((C, ROWS, CELLS), bf16),
            pltpu.VMEM((C, ROWS, MODES), bf16),
            pltpu.VMEM((C * ROWS, MODES), jnp.float32),
            pltpu.VMEM((C * SUB, C * SUB), jnp.float32),
            pltpu.VMEM((WIDTH, MODES), bf16),
            pltpu.VMEM((MODES, WIDTH), bf16),
            pltpu.SemaphoreType.DMA((CHUNKS,)),
            pltpu.SemaphoreType.DMA((CHUNKS,)),
            pltpu.SemaphoreType.DMA((CHUNKS,)),
        ],
        compiler_params=limit(53),
        name="slope_and_modes",
    )(
        slab,
        field,
        cotangent,
        point_weight,
        bias.reshape(C, 1),
        *mixed_parts,
    )

    full, send = pl.pallas_call(
        send_kernel,
        out_shape=(shaped(OWNED + SUB, MODES), shaped(dp, 3 * SUB, LANES)),
        compiler_params=limit(8),
        name="pieces_out",
    )(*reduce_parts(grad_parts), coef)
    back = pl.pallas_call(
        back_kernel,
        out_shape=shaped(OWNED, MODES),
        compiler_params=limit(8),
        name="back_modes",
    )(full, spec_weight)

    got = lax.all_to_all(send, "dp", 0, 0, tiled=True)
    two = flip(back, 2)
    back_parts = (back, flip(back, 1), two, flip(two, 1))
    copies, point_grad, bias_grad = pl.pallas_call(
        functools.partial(
            outer_kernel, 1.0 / math.sqrt(dp * N), 1.0 / math.sqrt(dp * N * N * N)
        ),
        out_shape=(shaped(dp, SUB, SUB, LANES), shaped(C, C), shaped(1, C)),
        compiler_params=limit(8),
        name="sample_sum",
    )(got)
    copies, *back_parts = lax.optimization_barrier((copies, *back_parts))
    owned = lax.all_to_all(copies, "dp", 0, 0, tiled=True)

    field_grad = pl.pallas_call(
        functools.partial(field_grad_kernel, 768),
        out_shape=jax.ShapeDtypeStruct(field.shape, bf16),
        in_specs=[SM, ANY] + [VM] * 5,
        out_specs=ANY,
        scratch_shapes=[
            pltpu.VMEM((N, MODES), jnp.float32),
            pltpu.VMEM((N, MODES), jnp.float32),
            pltpu.VMEM((C * SUB, C * SUB), bf16),
            pltpu.VMEM((M * C, MODES), jnp.float32),
            pltpu.VMEM((C, ROWS, CELLS), bf16),
            pltpu.VMEM((C, ROWS, CELLS), bf16),
            pltpu.VMEM((C, ROWS, MODES), bf16),
            pltpu.VMEM((MODES, WIDTH), bf16),
            pltpu.SemaphoreType.DMA((CHUNKS,)),
            pltpu.SemaphoreType.DMA((CHUNKS,)),
        ],
        compiler_params=limit(54),
        cost_estimate=pl.CostEstimate(
            flops=2 * C * ROWS * CELLS * (MODES + C * SUB),
            bytes_accessed=2 * C * ROWS * CELLS * 2,
            transcendentals=0,
        ),
        name="field_grad",
    )(slab, dpre, point_weight, *back_parts)

    spec_grad = pl.pallas_call(
        place_kernel,
        out_shape=shaped(M // GZ, C, C, MODES),
        in_specs=[VM],
        out_specs=ANY,
        scratch_shapes=[pltpu.SemaphoreType.DMA((dp,))],
        compiler_params=limit(8),
        name="place_pieces",
    )(owned)
    return field_grad, spec_grad, point_grad, bias_grad.reshape(C)


def solution(mesh):
    return jax.shard_map(
        shards,
        mesh=mesh,
        in_specs=(
            P("dp", None, "gz", None),
            P("dp", None, "gz", None),
            P("gz", None, None, None),
            P(),
            P(),
        ),
        out_specs=(P("dp", None, "gz", None), P("gz", None, None, None), P(), P()),
        check_vma=False,
    )
```
